128 devices in a mesh: segment: 4 (over y_lo, core), slab: 32 (over x, y_hi, z).
Axes of the slice: x: 4, y: 4 (y_hi: 2, y_lo: 2; y = y_hi * 2 + y_lo), z: 4, core: 2. Of those that a mesh axis runs over, the one named last changes fastest.
Arguments:
- raw_views: bfloat16 [2, 736, 4096], P(None, None, 'slab'), may hold values from -6 to 6
- tap_channel: int32 [736], replicated, may hold values from 0 to 734
- tap_view: int32 [736], replicated, may hold values from 0 to 2
- tap_weight: float32 [736], replicated, may hold values from 0 to 1
- batch_view: int32 [2], replicated, may hold values from 0 to 1151
- footprint: int32 [2, 32, 12], P(None, 'slab'), may hold values from 0 to 31, all different within a row
- plane_weight: bfloat16 [2, 32, 256, 128], P(None, 'slab'), may hold values from -0.5 to 0.5
Outputs:
- image: float32 [32, 256, 4096], P('slab', 'segment')
The draws below stay inside these ranges and needn't reach their ends.
Inputs may be any that keep to these rules, and one draw needn't show every extreme that they name: Each row of footprint names 12 distinct tiles.
All inputs are finite; a program needn't handle non-finite values.
Results may differ from the reference program's by a relative error of at most 0.0066.
Values may be sent and summed in bfloat16 or wider, within the bound.
No kernel may reach another device: no remote copies, remote signals or barrier semaphores. Data moves between devices by JAX's collectives and lax.ppermute only.
A program may use at most 128 MiB of HBM per device.

```python
import math
import jax
import jax.numpy as jnp
from jax import lax

CH = 736
ROWS = 64
PIX = 1024
YR = 4
VPT = 1152
VD = 2
MB = 2
TZ = 256
VDR = 128
VIEWS = 64
FOOT = 12
N_SLAB = 32


def touch_ends(result, own_key, smallest, largest):
    shape = result.shape
    index_at = [jax.random.randint(jax.random.fold_in(own_key, axis), (), 0, shape[axis]) for axis in range(len(shape))]
    result = result.at[tuple(index_at)].set(smallest)
    longest = shape.index(max(shape))
    index_at[longest] = (index_at[longest] + 1) % shape[longest]
    return result.at[tuple(index_at)].set(largest)


def level_of(key, extent, shards, smallest, top_value):
    def one(position, shards_of):
        draws = jax.random.uniform(jax.random.fold_in(jax.random.fold_in(key, 6), position), (shards_of,), jnp.float32, smallest / len(shards), top_value / len(shards))
        return jnp.repeat(jnp.exp(draws), extent[position] // shards_of).reshape((-1,) + (1,) * (len(extent) - position - 1))

    gain = one(*shards[0])
    for cut in shards[1:]:
        gain = gain * one(*cut)
    return gain


def distinct(key, rows, amount, top, lift):
    ranking = jax.random.permutation(jax.random.fold_in(key, 1), amount)
    pull = ranking
    for power in range(3):
        pull = pull * pull // amount
    pull = pull * lift // amount
    tickets = jax.random.randint(jax.random.fold_in(key, 2), (rows, amount), 0, 4096) + pull
    fixed_rows = jax.random.permutation(jax.random.fold_in(key, 3), rows)[jnp.arange(amount) % rows]
    tickets = jnp.where(jnp.arange(rows)[:, None] == fixed_rows[None, :], 1 << 14, tickets)
    priority = tickets * amount + jnp.arange(amount)
    return lax.top_k(priority.astype(jnp.int32), top)[1].astype(jnp.int32)


def bell_draw(key, dims, width, reach, shards=(), kind=jnp.bfloat16):
    values = width * jax.random.normal(key, dims, jnp.float32)
    if shards:
        values = values * level_of(key, dims, shards, -0.22, 0.18)
    return jnp.clip(values, -reach, reach).astype(kind)


def setup_inputs(seed: int = 0) -> dict:
    splits = jax.random.split(jax.random.key(seed), 8)
    raw_views = bell_draw(splits[0], (MB, CH, VIEWS * ROWS), 1.0, 6.0, ((2, 32),))
    tap_channel = touch_ends(jax.random.randint(splits[1], (CH,), 0, CH - 1), jax.random.fold_in(splits[1], 1), 0, (CH - 1) - 1).astype(jnp.int32)
    tap_view = touch_ends(jax.random.randint(splits[2], (CH,), 0, 3), jax.random.fold_in(splits[2], 1), 0, 2).astype(jnp.int32)
    tap_weight = jnp.clip(jax.random.uniform(splits[3], (CH,), jnp.float32, 0.0, 1.0), 0.0, 1.0)
    batch_view = jax.random.randint(splits[4], (MB,), 0, VPT).astype(jnp.int32)
    footprint = distinct(splits[5], MB * N_SLAB, N_SLAB, FOOT, 3072).reshape((MB, N_SLAB, FOOT))
    plane_weight = bell_draw(splits[6], (MB, N_SLAB, TZ, VDR), VDR ** -0.5, 0.5, ((1, 32),))
    return dict(raw_views=raw_views, tap_channel=tap_channel, tap_view=tap_view, tap_weight=tap_weight, batch_view=batch_view, footprint=footprint, plane_weight=plane_weight)


def ramp_matrix(channels):
    offset = jnp.arange(channels, dtype=jnp.int32)[:, None] - jnp.arange(channels, dtype=jnp.int32)[None, :]
    distance = offset.astype(jnp.float32)
    odd_mask = (offset % 2) != 0
    safe_dist = jnp.where(odd_mask, distance, 1.0)
    taps_full = jnp.where(odd_mask, -4.0 / (math.pi * math.pi * safe_dist * safe_dist), 0.0)
    taps_full = jnp.where(offset == 0, 1.0, taps_full)
    return taps_full.astype(jnp.bfloat16)


def rebin_views(extended, tap_channel, tap_view, tap_weight, det_rows, view_span):
    channels = extended.shape[0]
    shifted = jnp.concatenate([lax.slice_in_dim(extended, det_rows * offset, det_rows * offset + view_span, axis=1) for offset in range(3)], axis=0)
    source = tap_view.astype(jnp.int32) * channels + tap_channel.astype(jnp.int32)
    lower = jnp.take(shifted, source, axis=0).astype(jnp.float32)
    upper = jnp.take(shifted, source + 1, axis=0).astype(jnp.float32)
    weight_col = tap_weight[:, None]
    return ((1.0 - weight_col) * lower + weight_col * upper).astype(jnp.bfloat16)


def pixel_map(angle_index, slot_pos, slot_count, channels):
    theta = angle_index.astype(jnp.float32) * (2.0 * math.pi / VPT)
    pixels = jnp.arange(PIX * YR, dtype=jnp.int32)
    x_pos = (pixels % PIX).astype(jnp.float32) - (PIX / 2.0 - 0.5)
    y_base = (pixels // PIX).astype(jnp.float32) - (YR / 2.0 - 0.5)
    y_shift = (jnp.asarray(slot_pos).astype(jnp.float32) - (slot_count - 1) / 2.0) * (PIX / (4.0 * slot_count))
    y_pos = y_base + y_shift
    detector = (channels - 1) / 2.0 + (x_pos[None, :] * jnp.cos(theta)[:, None] + y_pos[None, :] * jnp.sin(theta)[:, None]) * (channels / PIX)
    centers = jnp.arange(channels, dtype=jnp.float32)
    return jnp.maximum(0.0, 1.0 - jnp.abs(detector[:, None, :] - centers[None, :, None])).astype(jnp.bfloat16)


def block_term(filtered, weights, angle_index, slot_pos, slot_count):
    channels = filtered.shape[0]
    view_count = angle_index.shape[0]
    mapping = pixel_map(angle_index, slot_pos, slot_count, channels)
    per_view = filtered.reshape(channels, view_count, ROWS).astype(jnp.float32)
    sampled = jnp.einsum("cvr,vcp->vrp", per_view, mapping.astype(jnp.float32)).astype(jnp.bfloat16)
    sampled = sampled.reshape(view_count * ROWS, -1)
    return jnp.dot(weights, sampled, preferred_element_type=jnp.float32)


def reference(raw_views, tap_channel, tap_view, tap_weight, batch_view, footprint, plane_weight):
    channels = raw_views.shape[1]
    view_cols = raw_views.shape[2]
    ramp_table = ramp_matrix(channels)
    image = jnp.zeros((N_SLAB, TZ, YR * PIX), jnp.float32)
    for batch_index in range(MB):
        padded = jnp.pad(raw_views[batch_index], ((0, 0), (ROWS, ROWS)))
        rebinned = rebin_views(padded, tap_channel, tap_view, tap_weight, ROWS, view_cols)
        filtered = jnp.dot(ramp_table, rebinned, preferred_element_type=jnp.float32).astype(jnp.bfloat16)
        batch_weight = plane_weight[batch_index]
        batch_foot = footprint[batch_index]
        first_view = batch_view[batch_index]

        def per_pair(pair, canvas):
            block = (pair // FOOT).astype(jnp.int32)
            slot_pos = (pair % FOOT).astype(jnp.int32)
            columns = lax.dynamic_slice_in_dim(filtered, block * (VD * ROWS), VD * ROWS, 1)
            angle_index = first_view + block * VD + jnp.arange(VD, dtype=jnp.int32)
            weights = lax.dynamic_index_in_dim(batch_weight, block, 0, keepdims=False)
            term = block_term(columns, weights, angle_index, slot_pos, FOOT)
            target = batch_foot[block, slot_pos].astype(jnp.int32)
            return canvas.at[target].add(term)

        image = lax.fori_loop(0, N_SLAB * FOOT, per_pair, image)
    return image
```

```python
import functools
import math

import jax
import jax.numpy as jnp
import numpy as np
from jax import lax
from jax.experimental import pallas as pl
from jax.experimental.pallas import tpu as pltpu
from jax.sharding import PartitionSpec as P

CH = 736
CHP = 768
ROWS = 64
COLS = 128
PIX = 1024
YR = 4
VPT = 1152
FOOT = 12
TZ = 256
PAY = CH + TZ + 16
STRIP = 128
STRIPS = PIX // STRIP
AXES = ("segment", "slab")
SCALE = CH / PIX
F32 = jnp.float32
BF16 = jnp.bfloat16


def linear(x, y, z, core):
    return ((y % 2) * 2 + core) * 32 + (x % 4) * 8 + (y // 2) * 4 + z % 4


def devices():
    for x in range(4):
        for y in range(4):
            for z in range(4):
                for core in range(2):
                    yield x, y, z, core


def home(slab, batch, core):
    x, y_hi, z = slab // 8, slab // 4 % 2, slab % 4
    return linear(x, batch if y_hi == 0 else 3 - batch, z, core)


def batch_of(y):
    return y % 2 ^ y // 2


def main_pairs():
    return [
        (home(x * 8 + core * 4 + z, batch_of(y), core), linear(x, y, z, core))
        for x, y, z, core in devices()
        if core != y // 2
    ]


def side_pairs(shift):
    pairs = []
    for x, y, z, core in devices():
        slab = x * 8 + core * 4 + z + shift
        if 0 <= slab < 32:
            pairs.append((home(slab, batch_of(y), y // 2), linear(x, y, z, core)))
    return pairs


def torus_pairs(even, odd):
    pairs = []
    for x, y, z, core in devices():
        dx, dz = odd if (x + z) % 2 else even
        pairs.append((linear(x + dx, y, z + dz, core), linear(x, y, z, core)))
    return pairs


A1, B1, C1 = ((2, 0), (0, 2)), ((0, 1), (1, 0)), ((0, -1), (-1, 0))
PHASE2 = (
    (0, (1, 0), (0, 1)),
    (0, (-1, 0), (0, -1)),
    (1, (0, 1), (1, 0)),
    (1, (0, -1), (-1, 0)),
    (0, (0, 2), (2, 0)),
    (1, (2, 0), (0, 2)),
)


def block_table():
    table = np.zeros((16, 16), np.int32)
    for x in range(4):
        for z in range(4):

            def first(px, pz):
                odd = (px + pz) % 2
                out = [(px, pz)]
                for offsets in (A1, B1, C1):
                    dx, dz = offsets[odd]
                    out.append((px + dx, pz + dz))
                return out

            found = first(x, z)
            for which, even, odd in PHASE2:
                dx, dz = odd if (x + z) % 2 else even
                source = first(x + dx, z + dz)
                found += source[:2] if which == 0 else source[2:]
            found = [(px % 4, pz % 4) for px, pz in found]
            assert len(set(found)) == 16
            table[x * 4 + z] = [px * 8 + pz for px, pz in found]
    return table


def ramp_matrix():
    row = lax.broadcasted_iota(jnp.int32, (CH, CHP), 0)
    col = lax.broadcasted_iota(jnp.int32, (CH, CHP), 1)
    offset = row - col
    distance = offset.astype(F32)
    odd_mask = offset % 2 != 0
    safe_dist = jnp.where(odd_mask, distance, 1.0)
    taps = jnp.where(odd_mask, -4.0 / (math.pi * math.pi * safe_dist * safe_dist), 0.0)
    taps = jnp.where(offset == 0, 1.0, taps)
    return jnp.where(col < CH, taps, 0.0).astype(BF16)


def filter_kernel(mine_ref, own_ref, other_ref, low_ref, high_ref, tap_ref, weight_ref, ramp_ref, out_ref, x_ref, r_ref):
    keep = mine_ref[0] != 0
    both = jnp.where(keep, own_ref[...], other_ref[...])
    raw = both[:CH]
    low = jnp.concatenate([low_ref[...], raw[:, :ROWS]], axis=1)
    high = jnp.concatenate([raw[:, ROWS:], high_ref[...]], axis=1)
    for tap, part in enumerate((low, raw, high)):
        up = jnp.concatenate([part[1:], part[:1]], axis=0)
        x_ref[tap, :CH, :COLS] = part
        x_ref[tap, :CH, COLS:] = up
        x_ref[tap, CH:, :] = jnp.zeros((CHP - CH, 2 * COLS), BF16)
    step = CH // 2
    for part in range(2):
        rows = pl.ds(part * step, step)
        total = jnp.zeros((step, 2 * COLS), F32)
        channel = lax.broadcasted_iota(jnp.int32, (step, CHP), 1)
        source = tap_ref[rows, :]
        for tap in range(3):
            pick = jnp.where(channel == source - tap * CH, 1.0, 0.0).astype(BF16)
            total += jnp.dot(pick, x_ref[tap], preferred_element_type=F32)
        weight = weight_ref[rows, :]
        r_ref[rows, :] = ((1.0 - weight) * total[:, :COLS] + weight * total[:, COLS:]).astype(BF16)
    r_ref[CH:, :] = jnp.zeros((CHP - CH, COLS), BF16)
    out_ref[:CH, :] = jnp.dot(ramp_ref[...], r_ref[...], preferred_element_type=F32).astype(BF16)
    out_ref[CH:, :] = both[CH:]


def project(first, base, names, tile_ref, cos_ref, sin_ref, acc_ref, g_ref, slot_ref):
    lane = lax.broadcasted_iota(jnp.int32, (16, COLS), 1)
    for index, block in enumerate(names):
        feet = block[CH + TZ :, :].astype(F32)
        row = lax.broadcasted_iota(jnp.int32, (16, COLS), 0)
        hit = jnp.logical_and(feet == tile_ref[0].astype(F32), row == 0)
        slot = jnp.sum(jnp.where(hit, lane + 1, 0).astype(F32)).astype(jnp.int32)
        slot_ref[index] = slot

        @pl.when(slot > 0)
        def _():
            weight = block[CH : CH + TZ, :]
            col = lax.broadcasted_iota(jnp.int32, (TZ, COLS), 1)
            zero = jnp.zeros_like(weight)
            for view in range(2):
                part = jnp.where((col < ROWS) == (view == 0), weight, zero)
                g_ref[index, :, pl.ds(view * TZ, TZ)] = lax.dot_general(
                    block[:CH, :], part, (((1,), (1,)), ((), ())), preferred_element_type=F32
                ).astype(BF16)

    if first:
        acc_ref[...] = jnp.zeros_like(acc_ref)

    def one_block(index, carry):
        slot = slot_ref[index]

        @pl.when(slot > 0)
        def _():
            shift = ((slot - 1).astype(F32) - (FOOT - 1) / 2.0) * (PIX / (4.0 * FOOT))
            y_first = shift - (YR / 2.0 - 0.5)
            cos = [cos_ref[2 * (base + index) + view] * SCALE for view in range(2)]
            sin = [sin_ref[2 * (base + index) + view] * SCALE for view in range(2)]
            x_iota = lax.broadcasted_iota(jnp.int32, (STRIP, COLS), 0).astype(F32)
            c_iota = lax.broadcasted_iota(jnp.int32, (STRIP, COLS), 1).astype(F32)
            slope = [x_iota * cos[view] - c_iota for view in range(2)]

            def one_strip(strip, inner):
                x_first = (strip * STRIP).astype(F32) - (PIX / 2.0 - 0.5)
                starts, parts = [], []
                for view in range(2):
                    u = (CH - 1) / 2.0 + x_first * cos[view] + y_first * sin[view]
                    low = (
                        u
                        + jnp.minimum(0.0, (STRIP - 1) * cos[view])
                        + jnp.minimum(0.0, (YR - 1) * sin[view])
                        - 1.5
                    )
                    start = jnp.clip(low, 0.0, float(CH - COLS)).astype(jnp.int32) // 16 * 16
                    offset = u - start.astype(F32)
                    starts.append(pl.multiple_of(start, 16))
                    rows = [
                        jnp.maximum(0.0, 1.0 - jnp.abs(slope[view] + (offset + y * sin[view]))).astype(BF16)
                        for y in range(YR)
                    ]
                    parts.append(jnp.concatenate(rows, axis=0))
                mapped = jnp.concatenate(parts, axis=1)
                right = jnp.concatenate(
                    [
                        g_ref[index, pl.ds(starts[view], COLS), pl.ds(view * TZ, TZ)]
                        for view in range(2)
                    ],
                    axis=0,
                )
                rows = pl.ds(pl.multiple_of(strip * (YR * STRIP), YR * STRIP), YR * STRIP)
                acc_ref[rows, :] += jnp.dot(mapped, right, preferred_element_type=F32)
                return inner

            lax.fori_loop(0, STRIPS, one_strip, 0)

        return carry

    lax.fori_loop(0, len(names), one_block, 0)


def first_kernel(tile_ref, cos_ref, sin_ref, b0, b1, b2, b3, acc_ref, g_ref, slot_ref):
    project(True, 0, [b0, b1, b2, b3], tile_ref, cos_ref, sin_ref, acc_ref, g_ref, slot_ref)


def middle_kernel(tile_ref, cos_ref, sin_ref, p0, p1, p2, p3, old_ref, acc_ref, g_ref, slot_ref):
    names = [pair.at[i] for pair in (p0, p1, p2, p3) for i in range(2)]
    acc_ref[...] = old_ref[...]
    project(False, 4, names, tile_ref, cos_ref, sin_ref, acc_ref, g_ref, slot_ref)


def last_kernel(tile_ref, cos_ref, sin_ref, p0, p1, old_ref, send_ref, keep_ref, acc_ref, g_ref, slot_ref):
    names = [pair.at[i] for pair in (p0, p1) for i in range(2)]
    acc_ref[...] = old_ref[...]
    project(False, 12, names, tile_ref, cos_ref, sin_ref, acc_ref, g_ref, slot_ref)
    core = tile_ref[1]

    def one_strip(strip, carry):
        for y in range(YR):
            rows = pl.ds(pl.multiple_of(strip * (YR * STRIP) + y * STRIP, STRIP), STRIP)
            turned = acc_ref[rows, :].T
            cols = pl.ds(pl.multiple_of(strip * STRIP + y * PIX, STRIP), STRIP)
            mine0 = jnp.where(core == 0, turned[:64], turned[64:128])
            mine1 = jnp.where(core == 0, turned[128:192], turned[192:])
            sent0 = jnp.where(core == 0, turned[64:128], turned[:64])
            sent1 = jnp.where(core == 0, turned[192:], turned[128:192])
            keep_ref[:64, cols] = mine0
            keep_ref[64:, cols] = mine1
            send_ref[:64, cols] = sent0.astype(BF16)
            send_ref[64:, cols] = sent1.astype(BF16)
        return carry

    lax.fori_loop(0, STRIPS, one_strip, 0)


def half_kernel(chip_ref, keep_ref, got_ref, send_ref, rest_ref):
    chip = chip_ref[0]
    mine = pl.ds(pl.multiple_of(chip * 64, 64), 64)
    theirs = pl.ds(pl.multiple_of((1 - chip) * 64, 64), 64)
    send_ref[...] = (keep_ref[theirs, :] + got_ref[theirs, :].astype(F32)).astype(BF16)
    rest_ref[...] = keep_ref[mine, :] + got_ref[mine, :].astype(F32)


def sum_kernel(rest_ref, got_ref, out_ref):
    out_ref[0] = rest_ref[...] + got_ref[...].astype(F32)


VMEM = pl.BlockSpec(memory_space=pltpu.VMEM)
SMEM = pl.BlockSpec(memory_space=pltpu.SMEM)


def shape(dims, dtype):
    return jax.ShapeDtypeStruct(dims, dtype)


def cost(flops, moved):
    return pl.CostEstimate(flops=flops, bytes_accessed=moved, transcendentals=0)


BLOCK_FLOPS = 2 * 4096 * 256 * 256 + 2 * CH * COLS * 512
PIXELS = YR * PIX


def shards(raw_views, tap_channel, tap_view, tap_weight, batch_view, footprint, plane_weight):
    segment = lax.axis_index("segment")
    slab = lax.axis_index("slab")
    chip, core = segment // 2, segment % 2
    x_pos, y_hi, z_pos = slab // 8, slab // 4 % 2, slab % 4
    batch = jnp.bitwise_xor(chip, y_hi)

    raw = lax.dynamic_index_in_dim(raw_views, batch, 0, keepdims=False)
    weights = lax.dynamic_index_in_dim(plane_weight, batch, 0, keepdims=False)[0]
    feet = lax.dynamic_index_in_dim(footprint, batch, 0, keepdims=False)
    feet = jnp.pad(feet.astype(BF16), ((0, 15), (0, COLS - FOOT)), constant_values=-1)
    own = jnp.concatenate([raw, weights, feet], axis=0)
    low = lax.ppermute(raw[:, ROWS:], AXES, side_pairs(-1))
    high = lax.ppermute(raw[:, :ROWS], AXES, side_pairs(1))
    other = lax.ppermute(own, AXES, main_pairs())

    source = (tap_view * CH + tap_channel)[:, None]
    payload = pl.pallas_call(
        filter_kernel,
        out_shape=shape((PAY, COLS), BF16),
        in_specs=[SMEM] + [VMEM] * 7,
        out_specs=VMEM,
        scratch_shapes=[pltpu.VMEM((3, CHP, 2 * COLS), BF16), pltpu.VMEM((CHP, COLS), BF16)],
        cost_estimate=cost(4 * 10**9, 4 * 10**6),
    )((core == y_hi).astype(jnp.int32)[None], own, other, low, high, source, tap_weight[:, None], ramp_matrix())

    got_a = lax.ppermute(payload, AXES, torus_pairs(*A1))
    got_b = lax.ppermute(payload, AXES, torus_pairs(*B1))
    got_c = lax.ppermute(payload, AXES, torus_pairs(*C1))
    pairs = (jnp.stack([payload, got_a]), jnp.stack([got_b, got_c]))
    got = [lax.ppermute(pairs[which], AXES, torus_pairs(even, odd)) for which, even, odd in PHASE2]

    blocks = lax.dynamic_index_in_dim(jnp.asarray(block_table()), x_pos * 4 + z_pos, 0, keepdims=False)
    first_view = lax.dynamic_index_in_dim(batch_view, batch, 0, keepdims=False)
    views = jnp.arange(32, dtype=jnp.int32)
    angle = first_view + 2 * (jnp.repeat(blocks, 2) + core * 4) + views % 2
    theta = angle.astype(F32) * (2.0 * math.pi / VPT)
    cos, sin = jnp.cos(theta), jnp.sin(theta)
    tile = jnp.where(jnp.arange(2) == 0, slab, core).astype(jnp.int32)

    def scratch(count):
        return [pltpu.VMEM((count, CH, 2 * TZ), BF16), pltpu.SMEM((count,), jnp.int32)]

    accumulator = shape((PIXELS, TZ), F32)
    total = pl.pallas_call(
        first_kernel,
        out_shape=accumulator,
        in_specs=[SMEM] * 3 + [VMEM] * 4,
        out_specs=VMEM,
        scratch_shapes=scratch(4),
        cost_estimate=cost(4 * BLOCK_FLOPS, 5 * 10**6),
    )(tile, cos, sin, payload, got_a, got_b, got_c)
    total = pl.pallas_call(
        middle_kernel,
        out_shape=accumulator,
        in_specs=[SMEM] * 3 + [VMEM] * 5,
        out_specs=VMEM,
        scratch_shapes=scratch(8),
        cost_estimate=cost(8 * BLOCK_FLOPS, 10 * 10**6),
    )(tile, cos, sin, *got[:4], total)
    send, keep = pl.pallas_call(
        last_kernel,
        out_shape=(shape((COLS, PIXELS), BF16), shape((COLS, PIXELS), F32)),
        in_specs=[SMEM] * 3 + [VMEM] * 3,
        out_specs=(VMEM, VMEM),
        scratch_shapes=[pltpu.VMEM((PIXELS, TZ), F32)] + scratch(4),
        cost_estimate=cost(4 * BLOCK_FLOPS, 9 * 10**6),
    )(tile, cos, sin, *got[4:], total)

    beside = [(s * 32 + t, (s ^ 1) * 32 + t) for s in range(4) for t in range(32)]
    across = [(s * 32 + t, (s ^ 2) * 32 + t) for s in range(4) for t in range(32)]
    swapped = lax.ppermute(send, AXES, beside)
    send, rest = pl.pallas_call(
        half_kernel,
        out_shape=(shape((64, PIXELS), BF16), shape((64, PIXELS), F32)),
        in_specs=[SMEM, VMEM, VMEM],
        out_specs=(VMEM, VMEM),
        cost_estimate=cost(10**6, 5 * 10**6),
    )(chip[None], keep, swapped)
    swapped = lax.ppermute(send, AXES, across)
    return pl.pallas_call(
        sum_kernel,
        out_shape=shape((1, 64, PIXELS), F32),
        in_specs=[VMEM, VMEM],
        out_specs=VMEM,
        cost_estimate=cost(10**6, 3 * 10**6),
    )(rest, swapped)


def solution(mesh):
    return jax.shard_map(
        shards,
        mesh=mesh,
        in_specs=(
            P(None, None, "slab"),
            P(),
            P(),
            P(),
            P(),
            P(None, "slab", None),
            P(None, "slab", None, None),
        ),
        out_specs=P("slab", "segment", None),
        check_vma=False,
    )
```

```python
import math

import jax
import jax.numpy as jnp
import numpy as np
from jax import lax
from jax.experimental import pallas as pl
from jax.experimental.pallas import tpu as pltpu
from jax.sharding import PartitionSpec as P

CH = 736
CHP = 768
ROWS = 64
COLS = 128
PIX = 1024
YR = 4
VPT = 1152
FOOT = 12
TZ = 256
PAY = CH + TZ + 16
STRIP = 128
STRIPS = PIX // STRIP
AXES = ("segment", "slab")
SCALE = CH / PIX
F32 = jnp.float32
BF16 = jnp.bfloat16


def linear(x, y, z, core):
    return ((y % 2) * 2 + core) * 32 + (x % 4) * 8 + (y // 2) * 4 + z % 4


def devices():
    for x in range(4):
        for y in range(4):
            for z in range(4):
                for core in range(2):
                    yield x, y, z, core


def home(slab, batch, core):
    x, y_hi, z = slab // 8, slab // 4 % 2, slab % 4
    return linear(x, batch if y_hi == 0 else 3 - batch, z, core)


def batch_of(y):
    return y % 2 ^ y // 2


def main_pairs():
    return [
        (home(x * 8 + core * 4 + z, batch_of(y), core), linear(x, y, z, core))
        for x, y, z, core in devices()
        if core != y // 2
    ]


def side_pairs(shift):
    pairs = []
    for x, y, z, core in devices():
        slab = x * 8 + core * 4 + z + shift
        if 0 <= slab < 32:
            pairs.append((home(slab, batch_of(y), y // 2), linear(x, y, z, core)))
    return pairs


def torus_pairs(even, odd):
    pairs = []
    for x, y, z, core in devices():
        dx, dz = odd if (x + z) % 2 else even
        pairs.append((linear(x + dx, y, z + dz, core), linear(x, y, z, core)))
    return pairs


A1, B1, C1 = ((2, 0), (0, 2)), ((0, 1), (1, 0)), ((0, -1), (-1, 0))
PHASE2 = (
    (0, (1, 0), (0, 1)),
    (0, (-1, 0), (0, -1)),
    (1, (0, 1), (1, 0)),
    (1, (0, -1), (-1, 0)),
    (0, (0, 2), (2, 0)),
    (1, (2, 0), (0, 2)),
)


def block_table():
    table = np.zeros((16, 16), np.int32)
    for x in range(4):
        for z in range(4):

            def first(px, pz):
                odd = (px + pz) % 2
                out = [(px, pz)]
                for offsets in (A1, B1, C1):
                    dx, dz = offsets[odd]
                    out.append((px + dx, pz + dz))
                return out

            found = first(x, z)
            for which, even, odd in PHASE2:
                dx, dz = odd if (x + z) % 2 else even
                source = first(x + dx, z + dz)
                found += source[:2] if which == 0 else source[2:]
            found = [(px % 4, pz % 4) for px, pz in found]
            assert len(set(found)) == 16
            table[x * 4 + z] = [px * 8 + pz for px, pz in found]
    return table


def ramp_matrix():
    row = lax.broadcasted_iota(jnp.int32, (CH, CHP), 0)
    col = lax.broadcasted_iota(jnp.int32, (CH, CHP), 1)
    offset = row - col
    distance = offset.astype(F32)
    odd_mask = offset % 2 != 0
    safe_dist = jnp.where(odd_mask, distance, 1.0)
    taps = jnp.where(odd_mask, -4.0 / (math.pi * math.pi * safe_dist * safe_dist), 0.0)
    taps = jnp.where(offset == 0, 1.0, taps)
    return jnp.where(col < CH, taps, 0.0).astype(BF16)


def filter_kernel(mine_ref, own_ref, other_ref, low_ref, high_ref, tap_ref, weight_ref, ramp_ref, out_ref, x_ref, r_ref):
    keep = mine_ref[0] != 0
    both = jnp.where(keep, own_ref[...], other_ref[...])
    raw = both[:CH]
    low = jnp.concatenate([low_ref[...], raw[:, :ROWS]], axis=1)
    high = jnp.concatenate([raw[:, ROWS:], high_ref[...]], axis=1)
    for tap, part in enumerate((low, raw, high)):
        up = jnp.concatenate([part[1:], part[:1]], axis=0)
        x_ref[tap, :CH, :COLS] = part
        x_ref[tap, :CH, COLS:] = up
        x_ref[tap, CH:, :] = jnp.zeros((CHP - CH, 2 * COLS), BF16)
    step = CH // 2
    for part in range(2):
        rows = pl.ds(part * step, step)
        total = jnp.zeros((step, 2 * COLS), F32)
        channel = lax.broadcasted_iota(jnp.int32, (step, CHP), 1)
        source = tap_ref[rows, :]
        for tap in range(3):
            pick = jnp.where(channel == source - tap * CH, 1.0, 0.0).astype(BF16)
            total += jnp.dot(pick, x_ref[tap], preferred_element_type=F32)
        weight = weight_ref[rows, :]
        r_ref[rows, :] = ((1.0 - weight) * total[:, :COLS] + weight * total[:, COLS:]).astype(BF16)
    r_ref[CH:, :] = jnp.zeros((CHP - CH, COLS), BF16)
    out_ref[:CH, :] = jnp.dot(ramp_ref[...], r_ref[...], preferred_element_type=F32).astype(BF16)
    out_ref[CH:, :] = both[CH:]


def project(first, base, names, tile_ref, cos_ref, sin_ref, acc_ref, g_ref, slot_ref):
    lane = lax.broadcasted_iota(jnp.int32, (16, COLS), 1)
    for index, block in enumerate(names):
        feet = block[CH + TZ :, :].astype(F32)
        row = lax.broadcasted_iota(jnp.int32, (16, COLS), 0)
        hit = jnp.logical_and(feet == tile_ref[0].astype(F32), row == 0)
        slot = jnp.sum(jnp.where(hit, lane + 1, 0).astype(F32)).astype(jnp.int32)
        slot_ref[index] = slot

        @pl.when(slot > 0)
        def _():
            weight = block[CH : CH + TZ, :]
            col = lax.broadcasted_iota(jnp.int32, (TZ, COLS), 1)
            zero = jnp.zeros_like(weight)
            for view in range(2):
                part = jnp.where((col < ROWS) == (view == 0), weight, zero)
                g_ref[index, :, pl.ds(view * TZ, TZ)] = lax.dot_general(
                    block[:CH, :], part, (((1,), (1,)), ((), ())), preferred_element_type=F32
                ).astype(BF16)

    if first:
        acc_ref[...] = jnp.zeros_like(acc_ref)

    def one_block(index, carry):
        slot = slot_ref[index]

        @pl.when(slot > 0)
        def _():
            shift = ((slot - 1).astype(F32) - (FOOT - 1) / 2.0) * (PIX / (4.0 * FOOT))
            y_first = shift - (YR / 2.0 - 0.5)
            cos = [cos_ref[2 * (base + index) + view] * SCALE for view in range(2)]
            sin = [sin_ref[2 * (base + index) + view] * SCALE for view in range(2)]
            x_iota = lax.broadcasted_iota(jnp.int32, (STRIP, COLS), 0).astype(F32)
            c_iota = lax.broadcasted_iota(jnp.int32, (STRIP, COLS), 1).astype(F32)
            slope = [x_iota * cos[view] - c_iota for view in range(2)]
            reach = [
                jnp.minimum(0.0, (STRIP - 1) * cos[view]) + jnp.minimum(0.0, (YR - 1) * sin[view]) - 1.5
                for view in range(2)
            ]
            zero, one = jnp.zeros((), BF16), jnp.ones((), BF16)

            for strip in range(STRIPS):
                x_first = strip * STRIP - (PIX / 2.0 - 0.5)
                starts, parts = [], []
                for view in range(2):
                    u = (CH - 1) / 2.0 + x_first * cos[view] + y_first * sin[view]
                    low = jnp.clip(u + reach[view], 0.0, float(CH - COLS)).astype(jnp.int32)
                    start = pl.multiple_of(lax.shift_left(lax.shift_right_logical(low, 4), 4), 16)
                    offset = u - start.astype(F32)
                    starts.append(start)
                    rows = []
                    for y in range(YR):
                        away = jnp.abs((slope[view] + (offset + y * sin[view])).astype(BF16))
                        rows.append(jnp.maximum(zero, one - away))
                    parts.append(jnp.concatenate(rows, axis=0))
                mapped = jnp.concatenate(parts, axis=1)
                right = jnp.concatenate(
                    [
                        g_ref[index, pl.ds(starts[view], COLS), pl.ds(view * TZ, TZ)]
                        for view in range(2)
                    ],
                    axis=0,
                )
                rows = pl.ds(strip * (YR * STRIP), YR * STRIP)
                acc_ref[rows, :] += jnp.dot(mapped, right, preferred_element_type=F32)

        return carry

    lax.fori_loop(0, len(names), one_block, 0)


def first_kernel(tile_ref, cos_ref, sin_ref, b0, b1, b2, b3, acc_ref, g_ref, slot_ref):
    project(True, 0, [b0, b1, b2, b3], tile_ref, cos_ref, sin_ref, acc_ref, g_ref, slot_ref)


def middle_kernel(tile_ref, cos_ref, sin_ref, p0, p1, p2, p3, old_ref, acc_ref, g_ref, slot_ref):
    names = [pair.at[i] for pair in (p0, p1, p2, p3) for i in range(2)]
    acc_ref[...] = old_ref[...]
    project(False, 4, names, tile_ref, cos_ref, sin_ref, acc_ref, g_ref, slot_ref)


def last_kernel(tile_ref, cos_ref, sin_ref, p0, p1, old_ref, send_ref, keep_ref, acc_ref, g_ref, slot_ref):
    names = [pair.at[i] for pair in (p0, p1) for i in range(2)]
    acc_ref[...] = old_ref[...]
    project(False, 12, names, tile_ref, cos_ref, sin_ref, acc_ref, g_ref, slot_ref)
    core = tile_ref[1]

    def one_strip(strip, carry):
        for y in range(YR):
            rows = pl.ds(pl.multiple_of(strip * (YR * STRIP) + y * STRIP, STRIP), STRIP)
            turned = acc_ref[rows, :].T
            cols = pl.ds(pl.multiple_of(strip * STRIP + y * PIX, STRIP), STRIP)
            mine0 = jnp.where(core == 0, turned[:64], turned[64:128])
            mine1 = jnp.where(core == 0, turned[128:192], turned[192:])
            sent0 = jnp.where(core == 0, turned[64:128], turned[:64])
            sent1 = jnp.where(core == 0, turned[192:], turned[128:192])
            keep_ref[:64, cols] = mine0
            keep_ref[64:, cols] = mine1
            send_ref[:64, cols] = sent0.astype(BF16)
            send_ref[64:, cols] = sent1.astype(BF16)
        return carry

    lax.fori_loop(0, STRIPS, one_strip, 0)


def half_kernel(chip_ref, keep_ref, got_ref, send_ref, rest_ref):
    chip = chip_ref[0]
    mine = pl.ds(pl.multiple_of(chip * 64, 64), 64)
    theirs = pl.ds(pl.multiple_of((1 - chip) * 64, 64), 64)
    send_ref[...] = (keep_ref[theirs, :] + got_ref[theirs, :].astype(F32)).astype(BF16)
    rest_ref[...] = keep_ref[mine, :] + got_ref[mine, :].astype(F32)


def sum_kernel(rest_ref, got_ref, out_ref):
    out_ref[0] = rest_ref[...] + got_ref[...].astype(F32)


VMEM = pl.BlockSpec(memory_space=pltpu.VMEM)
SMEM = pl.BlockSpec(memory_space=pltpu.SMEM)


def shape(dims, dtype):
    return jax.ShapeDtypeStruct(dims, dtype)


def cost(flops, moved):
    return pl.CostEstimate(flops=flops, bytes_accessed=moved, transcendentals=0)


LIMIT = 24 * 2**20
BLOCK_FLOPS = 2 * 4096 * 256 * 256 + 2 * CH * COLS * 512
PIXELS = YR * PIX


def shards(raw_views, tap_channel, tap_view, tap_weight, batch_view, footprint, plane_weight):
    segment = lax.axis_index("segment")
    slab = lax.axis_index("slab")
    chip, core = segment // 2, segment % 2
    x_pos, y_hi, z_pos = slab // 8, slab // 4 % 2, slab % 4
    batch = jnp.bitwise_xor(chip, y_hi)

    raw = lax.dynamic_index_in_dim(raw_views, batch, 0, keepdims=False)
    weights = lax.dynamic_index_in_dim(plane_weight, batch, 0, keepdims=False)[0]
    feet = lax.dynamic_index_in_dim(footprint, batch, 0, keepdims=False)
    feet = jnp.pad(feet.astype(BF16), ((0, 15), (0, COLS - FOOT)), constant_values=-1)
    own = jnp.concatenate([raw, weights, feet], axis=0)
    low = lax.ppermute(raw[:, ROWS:], AXES, side_pairs(-1))
    high = lax.ppermute(raw[:, :ROWS], AXES, side_pairs(1))
    other = lax.ppermute(own, AXES, main_pairs())

    source = (tap_view * CH + tap_channel)[:, None]
    payload = pl.pallas_call(
        filter_kernel,
        out_shape=shape((PAY, COLS), BF16),
        in_specs=[SMEM] + [VMEM] * 7,
        out_specs=VMEM,
        scratch_shapes=[pltpu.VMEM((3, CHP, 2 * COLS), BF16), pltpu.VMEM((CHP, COLS), BF16)],
        compiler_params=pltpu.CompilerParams(vmem_limit_bytes=LIMIT),
        cost_estimate=cost(4 * 10**9, 4 * 10**6),
    )((core == y_hi).astype(jnp.int32)[None], own, other, low, high, source, tap_weight[:, None], ramp_matrix())

    got_a = lax.ppermute(payload, AXES, torus_pairs(*A1))
    got_b = lax.ppermute(payload, AXES, torus_pairs(*B1))
    got_c = lax.ppermute(payload, AXES, torus_pairs(*C1))
    pairs = (jnp.stack([payload, got_a]), jnp.stack([got_b, got_c]))
    got = [lax.ppermute(pairs[which], AXES, torus_pairs(even, odd)) for which, even, odd in PHASE2]

    blocks = lax.dynamic_index_in_dim(jnp.asarray(block_table()), x_pos * 4 + z_pos, 0, keepdims=False)
    first_view = lax.dynamic_index_in_dim(batch_view, batch, 0, keepdims=False)
    views = jnp.arange(32, dtype=jnp.int32)
    angle = first_view + 2 * (jnp.repeat(blocks, 2) + core * 4) + views % 2
    theta = angle.astype(F32) * (2.0 * math.pi / VPT)
    cos, sin = jnp.cos(theta), jnp.sin(theta)
    tile = jnp.where(jnp.arange(2) == 0, slab, core).astype(jnp.int32)

    def scratch(count):
        return [pltpu.VMEM((count, CH, 2 * TZ), BF16), pltpu.SMEM((count,), jnp.int32)]

    accumulator = shape((PIXELS, TZ), F32)
    total = pl.pallas_call(
        first_kernel,
        out_shape=accumulator,
        in_specs=[SMEM] * 3 + [VMEM] * 4,
        out_specs=VMEM,
        scratch_shapes=scratch(4),
        compiler_params=pltpu.CompilerParams(vmem_limit_bytes=LIMIT),
        cost_estimate=cost(4 * BLOCK_FLOPS, 5 * 10**6),
    )(tile, cos, sin, payload, got_a, got_b, got_c)
    total = pl.pallas_call(
        middle_kernel,
        out_shape=accumulator,
        in_specs=[SMEM] * 3 + [VMEM] * 5,
        out_specs=VMEM,
        scratch_shapes=scratch(8),
        compiler_params=pltpu.CompilerParams(vmem_limit_bytes=LIMIT),
        cost_estimate=cost(8 * BLOCK_FLOPS, 10 * 10**6),
    )(tile, cos, sin, *got[:4], total)
    send, keep = pl.pallas_call(
        last_kernel,
        out_shape=(shape((COLS, PIXELS), BF16), shape((COLS, PIXELS), F32)),
        in_specs=[SMEM] * 3 + [VMEM] * 3,
        out_specs=(VMEM, VMEM),
        scratch_shapes=[pltpu.VMEM((PIXELS, TZ), F32)] + scratch(4),
        compiler_params=pltpu.CompilerParams(vmem_limit_bytes=LIMIT),
        cost_estimate=cost(4 * BLOCK_FLOPS, 9 * 10**6),
    )(tile, cos, sin, *got[4:], total)

    beside = [(s * 32 + t, (s ^ 1) * 32 + t) for s in range(4) for t in range(32)]
    across = [(s * 32 + t, (s ^ 2) * 32 + t) for s in range(4) for t in range(32)]
    swapped = lax.ppermute(send, AXES, beside)
    send, rest = pl.pallas_call(
        half_kernel,
        out_shape=(shape((64, PIXELS), BF16), shape((64, PIXELS), F32)),
        in_specs=[SMEM, VMEM, VMEM],
        out_specs=(VMEM, VMEM),
        compiler_params=pltpu.CompilerParams(vmem_limit_bytes=LIMIT),
        cost_estimate=cost(10**6, 5 * 10**6),
    )(chip[None], keep, swapped)
    swapped = lax.ppermute(send, AXES, across)
    return pl.pallas_call(
        sum_kernel,
        out_shape=shape((1, 64, PIXELS), F32),
        in_specs=[VMEM, VMEM],
        out_specs=VMEM,
        compiler_params=pltpu.CompilerParams(vmem_limit_bytes=LIMIT),
        cost_estimate=cost(10**6, 3 * 10**6),
    )(rest, swapped)


def solution(mesh):
    return jax.shard_map(
        shards,
        mesh=mesh,
        in_specs=(
            P(None, None, "slab"),
            P(),
            P(),
            P(),
            P(),
            P(None, "slab", None),
            P(None, "slab", None, None),
        ),
        out_specs=P("slab", "segment", None),
        check_vma=False,
    )
```

```python
import functools
import math

import jax
import jax.numpy as jnp
import numpy as np
from jax import lax
from jax.experimental import pallas as pl
from jax.experimental.pallas import tpu as pltpu
from jax.sharding import PartitionSpec as P

CH = 736
CHP = 768
ROWS = 64
COLS = 128
PIX = 1024
YR = 4
VPT = 1152
FOOT = 12
TZ = 256
PAY = CH + TZ + 16
STRIP = 128
STRIPS = PIX // STRIP
AXES = ("segment", "slab")
SCALE = CH / PIX
F32 = jnp.float32
BF16 = jnp.bfloat16


def linear(x, y, z, core):
    return ((y % 2) * 2 + core) * 32 + (x % 4) * 8 + (y // 2) * 4 + z % 4


def devices():
    for x in range(4):
        for y in range(4):
            for z in range(4):
                for core in range(2):
                    yield x, y, z, core


def home(slab, batch, core):
    x, y_hi, z = slab // 8, slab // 4 % 2, slab % 4
    return linear(x, batch if y_hi == 0 else 3 - batch, z, core)


def batch_of(y):
    return y % 2 ^ y // 2


def main_pairs():
    return [
        (home(x * 8 + core * 4 + z, batch_of(y), core), linear(x, y, z, core))
        for x, y, z, core in devices()
        if core != y // 2
    ]


def side_pairs(shift):
    pairs = []
    for x, y, z, core in devices():
        slab = x * 8 + core * 4 + z + shift
        if 0 <= slab < 32:
            pairs.append((home(slab, batch_of(y), y // 2), linear(x, y, z, core)))
    return pairs


def torus_pairs(even, odd):
    pairs = []
    for x, y, z, core in devices():
        dx, dz = odd if (x + z) % 2 else even
        pairs.append((linear(x + dx, y, z + dz, core), linear(x, y, z, core)))
    return pairs


A1, B1, C1 = ((2, 0), (0, 2)), ((0, 1), (1, 0)), ((0, -1), (-1, 0))
NEAR = (
    (0, (1, 0), (0, 1)),
    (0, (-1, 0), (0, -1)),
    (1, (0, 1), (1, 0)),
    (1, (0, -1), (-1, 0)),
)
FAR = ((0, (0, 1), (1, 0)), (3, (-1, 0), (0, -1)))


def block_table():
    table = np.zeros((16, 16), np.int32)
    for x in range(4):
        for z in range(4):

            def first(px, pz):
                odd = (px + pz) % 2
                out = [(px, pz)]
                for offsets in (A1, B1, C1):
                    dx, dz = offsets[odd]
                    out.append((px + dx, pz + dz))
                return out

            found = first(x, z)

            def second(px, pz, arrival):
                which, even, odd = NEAR[arrival]
                dx, dz = odd if (px + pz) % 2 else even
                source = first(px + dx, pz + dz)
                return source[:2] if which == 0 else source[2:]

            for arrival in range(4):
                found += second(x, z, arrival)
            for arrival, even, odd in FAR:
                dx, dz = odd if (x + z) % 2 else even
                found += second(x + dx, z + dz, arrival)
            found = [(px % 4, pz % 4) for px, pz in found]
            assert len(set(found)) == 16
            table[x * 4 + z] = [px * 8 + pz for px, pz in found]
    return table


def ramp_matrix():
    distance = np.arange(CH)[:, None] - np.arange(CHP)[None, :]
    odd = distance % 2 != 0
    taps = np.where(odd, -4.0 / (math.pi**2 * np.where(odd, distance, 1) ** 2.0), 0.0)
    taps = np.where(distance == 0, 1.0, taps) * (np.arange(CHP) < CH)
    return jnp.asarray(taps.astype(np.float32).astype(BF16))


def packed(view):
    return jnp.concatenate([view[: CH // 2], view[CH // 2 :]], axis=1)


def unpacked(ref):
    return jnp.concatenate([ref[:, :ROWS], ref[:, ROWS:]], axis=0)


def column(line):
    return jnp.broadcast_to(line.reshape(1, CH), (8, CH)).T[:, :1]


def message_kernel(batch_ref, feet_hbm, raw_hbm, weight_hbm, own_ref, last_ref, first_ref, feet_ref, sem):
    batch = batch_ref[0]
    copies = [
        pltpu.make_async_copy(raw_hbm.at[batch], own_ref.at[pl.ds(0, CH)], sem.at[0]),
        pltpu.make_async_copy(weight_hbm.at[batch, 0], own_ref.at[pl.ds(CH, TZ)], sem.at[1]),
        pltpu.make_async_copy(feet_hbm, feet_ref, sem.at[2]),
    ]
    for copy in copies:
        copy.start()
    for copy in copies:
        copy.wait()
    row = lax.broadcasted_iota(jnp.int32, (16, COLS), 0)
    lane = lax.broadcasted_iota(jnp.int32, (16, COLS), 1)
    feet = jnp.full((16, COLS), -1.0, F32)
    for slot in range(FOOT):
        here = jnp.logical_and(row == 0, lane == slot)
        feet = jnp.where(here, feet_ref[batch, 0, slot].astype(F32), feet)
    own_ref[CH + TZ :, :] = feet.astype(BF16)
    raw = own_ref[:CH, :]
    last_ref[...] = packed(raw[:, ROWS:])
    first_ref[...] = packed(raw[:, :ROWS])


def pair_kernel(one_ref, two_ref, *refs):
    out_ref = refs[-1]
    out_ref[0] = one_ref[...]
    out_ref[1] = two_ref[...]


def filter_kernel(mine_ref, own_ref, other_ref, low_ref, high_ref, channel_ref, view_ref, weight_ref, ramp_ref, out_ref, x_ref, r_ref):
    keep = mine_ref[0] != 0
    both = jnp.where(keep, own_ref[...], other_ref[...])
    raw = both[:CH]
    low = jnp.concatenate([unpacked(low_ref), raw[:, :ROWS]], axis=1)
    high = jnp.concatenate([raw[:, ROWS:], unpacked(high_ref)], axis=1)
    for tap, part in enumerate((low, raw, high)):
        up = jnp.concatenate([part[1:], part[:1]], axis=0)
        x_ref[tap, :CH, :COLS] = part
        x_ref[tap, :CH, COLS:] = up
        x_ref[tap, CH:, :] = jnp.zeros((CHP - CH, 2 * COLS), BF16)
    sources = column(view_ref[...] * CH + channel_ref[...])
    weights = column(weight_ref[...])
    step = CH // 2
    for part in range(2):
        rows = pl.ds(part * step, step)
        total = jnp.zeros((step, 2 * COLS), F32)
        channel = lax.broadcasted_iota(jnp.int32, (step, CHP), 1)
        source = sources[part * step : (part + 1) * step]
        for tap in range(3):
            pick = jnp.where(channel == source - tap * CH, 1.0, 0.0).astype(BF16)
            total += jnp.dot(pick, x_ref[tap], preferred_element_type=F32)
        weight = weights[part * step : (part + 1) * step]
        r_ref[rows, :] = ((1.0 - weight) * total[:, :COLS] + weight * total[:, COLS:]).astype(BF16)
    r_ref[CH:, :] = jnp.zeros((CHP - CH, COLS), BF16)
    out_ref[:CH, :] = jnp.dot(ramp_ref[...], r_ref[...], preferred_element_type=F32).astype(BF16)
    out_ref[CH:, :] = both[CH:]


def weigh(names, tile_ref, g_ref, slot_ref):
    lane = lax.broadcasted_iota(jnp.int32, (16, COLS), 1)
    row = lax.broadcasted_iota(jnp.int32, (16, COLS), 0)
    col = lax.broadcasted_iota(jnp.int32, (TZ, COLS), 1)
    for index, block in enumerate(names):
        feet = block[CH + TZ :, :].astype(F32)
        hit = jnp.logical_and(feet == tile_ref[0].astype(F32), row == 0)
        slot = jnp.sum(jnp.where(hit, lane + 1, 0).astype(F32)).astype(jnp.int32)
        slot_ref[index] = slot

        @pl.when(slot > 0)
        def _():
            weight = block[CH : CH + TZ, :]
            zero = jnp.zeros_like(weight)
            for view in range(2):
                part = jnp.where((col < ROWS) == (view == 0), weight, zero)
                g_ref[index, :, pl.ds(view * TZ, TZ)] = lax.dot_general(
                    block[:CH, :], part, (((1,), (1,)), ((), ())), preferred_element_type=F32
                ).astype(BF16)


def project(base, count, strips, cos_ref, sin_ref, acc_ref, g_ref, slot_ref):
    def one_block(index, carry):
        slot = slot_ref[index]

        @pl.when(slot > 0)
        def _():
            shift = ((slot - 1).astype(F32) - (FOOT - 1) / 2.0) * (PIX / (4.0 * FOOT))
            y_first = shift - (YR / 2.0 - 0.5)
            cos = [cos_ref[2 * (base + index) + view] * SCALE for view in range(2)]
            sin = [sin_ref[2 * (base + index) + view] * SCALE for view in range(2)]
            x_iota = lax.broadcasted_iota(jnp.int32, (STRIP, COLS), 0).astype(F32)
            c_iota = lax.broadcasted_iota(jnp.int32, (STRIP, COLS), 1).astype(F32)
            slope = [x_iota * cos[view] - c_iota for view in range(2)]
            reach = [
                jnp.minimum(0.0, (STRIP - 1) * cos[view]) + jnp.minimum(0.0, (YR - 1) * sin[view]) - 1.5
                for view in range(2)
            ]
            zero, one = jnp.zeros((), BF16), jnp.ones((), BF16)
            for place, strip in enumerate(strips):
                x_first = strip * STRIP - (PIX / 2.0 - 0.5)
                starts, parts = [], []
                for view in range(2):
                    u = (CH - 1) / 2.0 + x_first * cos[view] + y_first * sin[view]
                    low = jnp.clip(u + reach[view], 0.0, float(CH - COLS)).astype(jnp.int32)
                    start = pl.multiple_of(lax.shift_left(lax.shift_right_logical(low, 4), 4), 16)
                    offset = u - start.astype(F32)
                    starts.append(start)
                    rows = []
                    for y in range(YR):
                        away = jnp.abs((slope[view] + (offset + y * sin[view])).astype(BF16))
                        rows.append(jnp.maximum(zero, one - away))
                    parts.append(jnp.concatenate(rows, axis=0))
                mapped = jnp.concatenate(parts, axis=1)
                right = jnp.concatenate(
                    [
                        g_ref[index, pl.ds(starts[view], COLS), pl.ds(view * TZ, TZ)]
                        for view in range(2)
                    ],
                    axis=0,
                )
                rows = pl.ds(place * (YR * STRIP), YR * STRIP)
                acc_ref[rows, :] += jnp.dot(mapped, right, preferred_element_type=F32)

        return carry

    lax.fori_loop(0, count, one_block, 0)


def first_kernel(tile_ref, cos_ref, sin_ref, b0, b1, b2, b3, acc_ref, g_ref, slot_ref):
    weigh([b0, b1, b2, b3], tile_ref, g_ref, slot_ref)
    acc_ref[...] = jnp.zeros_like(acc_ref)
    project(0, 4, range(STRIPS), cos_ref, sin_ref, acc_ref, g_ref, slot_ref)


def middle_kernel(tile_ref, cos_ref, sin_ref, p0, p1, p2, p3, old_ref, acc_ref, g_ref, slot_ref):
    names = [pair.at[i] for pair in (p0, p1, p2, p3) for i in range(2)]
    weigh(names, tile_ref, g_ref, slot_ref)
    acc_ref[...] = old_ref[...]
    project(4, 8, range(STRIPS), cos_ref, sin_ref, acc_ref, g_ref, slot_ref)


def turn(core, acc_ref, send_ref, keep_ref):
    width = PIX // 2

    def one_strip(strip, carry):
        for y in range(YR):
            rows = pl.ds(pl.multiple_of(strip * (YR * STRIP) + y * STRIP, STRIP), STRIP)
            turned = acc_ref[rows, :].T
            cols = pl.ds(pl.multiple_of(strip * STRIP + y * width, STRIP), STRIP)
            keep_ref[:64, cols] = jnp.where(core == 0, turned[:64], turned[64:128])
            keep_ref[64:, cols] = jnp.where(core == 0, turned[128:192], turned[192:])
            send_ref[:64, cols] = jnp.where(core == 0, turned[64:128], turned[:64]).astype(BF16)
            send_ref[64:, cols] = jnp.where(core == 0, turned[192:], turned[128:192]).astype(BF16)
        return carry

    lax.fori_loop(0, STRIPS // 2, one_strip, 0)


def left_kernel(
    tile_ref, cos_ref, sin_ref, p0, p1, old_ref, send_ref, keep_ref, g_ref, slot_ref, acc_ref
):
    names = [pair.at[i] for pair in (p0, p1) for i in range(2)]
    weigh(names, tile_ref, g_ref, slot_ref)
    acc_ref[...] = old_ref[: PIXELS // 2, :]
    project(12, 4, range(STRIPS // 2), cos_ref, sin_ref, acc_ref, g_ref, slot_ref)
    turn(tile_ref[1], acc_ref, send_ref, keep_ref)


def right_kernel(
    tile_ref, cos_ref, sin_ref, slot_ref, g_ref, old_ref, send_ref, keep_ref, acc_ref
):
    acc_ref[...] = old_ref[PIXELS // 2 :, :]
    project(12, 4, range(STRIPS // 2, STRIPS), cos_ref, sin_ref, acc_ref, g_ref, slot_ref)
    turn(tile_ref[1], acc_ref, send_ref, keep_ref)


def half_kernel(chip_ref, keep_ref, got_ref, *refs):
    send_ref, rest_ref = refs[-2:]
    chip = chip_ref[0]
    mine = pl.ds(pl.multiple_of(chip * 64, 64), 64)
    theirs = pl.ds(pl.multiple_of((1 - chip) * 64, 64), 64)
    send_ref[...] = (keep_ref[theirs, :] + got_ref[theirs, :].astype(F32)).astype(BF16)
    rest_ref[...] = keep_ref[mine, :] + got_ref[mine, :].astype(F32)


def sum_kernel(half, rest_ref, got_ref, *refs):
    out_ref, sum_ref, sem = refs[-3:]
    width = PIX // 2
    copies = []
    for y in range(YR):
        cols = pl.ds(y * width, width)
        sum_ref[:, cols] = rest_ref[:, cols] + got_ref[:, cols].astype(F32)
        place = out_ref.at[0, :, pl.ds(y * PIX + half * width, width)]
        copies.append(pltpu.make_async_copy(sum_ref.at[:, cols], place, sem.at[y]))
    for copy in copies:
        copy.start()
    for copy in copies:
        copy.wait()


VMEM = pl.BlockSpec(memory_space=pltpu.VMEM)
SMEM = pl.BlockSpec(memory_space=pltpu.SMEM)
HBM = pl.BlockSpec(memory_space=pltpu.HBM)
LATER = pl.BlockSpec(memory_space=pl.ANY)


def stay(array):
    return pltpu.with_memory_space_constraint(array, pltpu.HBM)


def shape(dims, dtype):
    return jax.ShapeDtypeStruct(dims, dtype)


def cost(flops, moved):
    return pl.CostEstimate(flops=flops, bytes_accessed=moved, transcendentals=0)


LIMIT = 24 * 2**20
BLOCK_FLOPS = 2 * 4096 * 256 * 256 + 2 * CH * COLS * 512
PIXELS = YR * PIX


def shards(raw_views, tap_channel, tap_view, tap_weight, batch_view, footprint, plane_weight):
    segment = lax.axis_index("segment")
    slab = lax.axis_index("slab")
    chip, core = segment // 2, segment % 2
    x_pos, y_hi, z_pos = slab // 8, slab // 4 % 2, slab % 4
    batch = jnp.bitwise_xor(chip, y_hi)

    def call(kernel, out_shape, in_specs, *operands, scratch=(), work=(10**5, 10**6), limit=LIMIT):
        many = isinstance(out_shape, tuple)
        return pl.pallas_call(
            kernel,
            out_shape=out_shape,
            in_specs=in_specs,
            out_specs=tuple(SMEM if o.dtype == jnp.int32 else VMEM for o in out_shape) if many else VMEM,
            scratch_shapes=list(scratch),
            compiler_params=pltpu.CompilerParams(vmem_limit_bytes=limit),
            cost_estimate=cost(*work),
        )(*operands)

    own, last, first = call(
        message_kernel,
        (shape((PAY, COLS), BF16), shape((CH // 2, COLS), BF16), shape((CH // 2, COLS), BF16)),
        [SMEM, HBM, HBM, HBM],
        batch[None],
        stay(footprint),
        stay(raw_views),
        stay(plane_weight),
        scratch=[pltpu.SMEM((2, 1, FOOT), jnp.int32), pltpu.SemaphoreType.DMA((3,))],
    )
    other = lax.ppermute(own, AXES, main_pairs())
    low = lax.ppermute(last, AXES, side_pairs(-1))
    high = lax.ppermute(first, AXES, side_pairs(1))

    payload = call(
        filter_kernel,
        shape((PAY, COLS), BF16),
        [SMEM] + [VMEM] * 8,
        (core == y_hi).astype(jnp.int32)[None],
        own,
        other,
        low,
        high,
        stay(tap_channel),
        stay(tap_view),
        stay(tap_weight),
        stay(ramp_matrix()),
        scratch=[pltpu.VMEM((3, CHP, 2 * COLS), BF16), pltpu.VMEM((CHP, COLS), BF16)],
        work=(4 * 10**9, 4 * 10**6),
    )

    payload, batch_view = lax.optimization_barrier((payload, batch_view))
    got_a = lax.ppermute(payload, AXES, torus_pairs(*A1))
    got_b = lax.ppermute(payload, AXES, torus_pairs(*B1))
    got_c = lax.ppermute(payload, AXES, torus_pairs(*C1))
    blocks = lax.dynamic_index_in_dim(jnp.asarray(block_table()), x_pos * 4 + z_pos, 0, keepdims=False)
    first_view = lax.dynamic_index_in_dim(batch_view, batch, 0, keepdims=False)
    views = jnp.arange(32, dtype=jnp.int32)
    angle = first_view + 2 * (jnp.repeat(blocks, 2) + core * 4) + views % 2
    theta = angle.astype(F32) * (2.0 * math.pi / VPT)
    cos, sin = jnp.cos(theta), jnp.sin(theta)
    tile = jnp.where(jnp.arange(2) == 0, slab, core).astype(jnp.int32)

    two = shape((2, PAY, COLS), BF16)
    pairs = (
        call(pair_kernel, two, [VMEM, VMEM], payload, got_a),
        call(pair_kernel, two, [VMEM, VMEM] + [SMEM] * 3, got_b, got_c, tile, cos, sin),
    )
    near = [lax.ppermute(pairs[which], AXES, torus_pairs(even, odd)) for which, even, odd in NEAR]

    def scratch(count):
        return [pltpu.VMEM((count, CH, 2 * TZ), BF16), pltpu.SMEM((count,), jnp.int32)]

    accumulator = shape((PIXELS, TZ), F32)
    half = (shape((COLS, PIXELS // 2), BF16), shape((COLS, PIXELS // 2), F32))
    half_scratch = [pltpu.VMEM((PIXELS // 2, TZ), F32)]
    total = call(
        first_kernel, accumulator, [SMEM] * 3 + [VMEM] * 4,
        tile, cos, sin, payload, got_a, got_b, got_c,
        scratch=scratch(4), work=(4 * BLOCK_FLOPS, 5 * 10**6),
    )
    *passed, total = lax.optimization_barrier((*(near[arrival] for arrival, _, _ in FAR), total))
    far = [lax.ppermute(part, AXES, torus_pairs(even, odd)) for part, (_, even, odd) in zip(passed, FAR)]
    total = call(
        middle_kernel, accumulator, [SMEM] * 3 + [VMEM] * 5,
        tile, cos, sin, *near, total,
        scratch=scratch(8), work=(8 * BLOCK_FLOPS, 10**7),
    )
    send_left, keep_left, kept, slots = call(
        left_kernel,
        half + (shape((4, CH, 2 * TZ), BF16), shape((4,), jnp.int32)),
        [SMEM] * 3 + [VMEM] * 3,
        tile, cos, sin, *far, total,
        scratch=half_scratch, work=(2 * BLOCK_FLOPS, 9 * 10**6),
    )
    send_right, keep_right = call(
        right_kernel,
        half,
        [SMEM] * 4 + [VMEM] * 2,
        tile, cos, sin, slots, kept, total,
        scratch=half_scratch, work=(2 * BLOCK_FLOPS, 9 * 10**6),
    )

    beside = [(s * 32 + t, (s ^ 1) * 32 + t) for s in range(4) for t in range(32)]
    across = [(s * 32 + t, (s ^ 2) * 32 + t) for s in range(4) for t in range(32)]
    ends, before = [], []
    for send, keep in ((send_left, keep_left), (send_right, keep_right)):
        swapped = lax.ppermute(send, AXES, beside)
        send, rest = call(
            half_kernel,
            (shape((64, PIXELS // 2), BF16), shape((64, PIXELS // 2), F32)),
            [SMEM, VMEM, VMEM] + [LATER] * len(before),
            chip[None], keep, swapped, *before,
        )
        before = [send]
        ends.append((rest, lax.ppermute(send, AXES, across)))
    image = None
    for half, (rest, swapped) in enumerate(ends):
        image = pl.pallas_call(
            functools.partial(sum_kernel, half),
            out_shape=shape((1, 64, PIXELS), F32),
            in_specs=[VMEM, VMEM] + [LATER] * half,
            out_specs=LATER,
            scratch_shapes=[pltpu.VMEM((64, PIXELS // 2), F32), pltpu.SemaphoreType.DMA((YR,))],
            input_output_aliases={2: 0} if half else {},
            compiler_params=pltpu.CompilerParams(vmem_limit_bytes=LIMIT),
            cost_estimate=cost(10**5, 10**6),
        )(rest, swapped, *([image] * half))
    return image


def solution(mesh):
    return jax.shard_map(
        shards,
        mesh=mesh,
        in_specs=(
            P(None, None, "slab"),
            P(),
            P(),
            P(),
            P(),
            P(None, "slab", None),
            P(None, "slab", None, None),
        ),
        out_specs=P("slab", "segment", None),
        check_vma=False,
    )
```

```python
import functools
import math

import jax
import jax.numpy as jnp
import numpy as np
from jax import lax
from jax.experimental import pallas as pl
from jax.experimental.pallas import tpu as pltpu
from jax.sharding import PartitionSpec as P

CH = 736
CHP = 768
ROWS = 64
COLS = 128
PIX = 1024
YR = 4
VPT = 1152
FOOT = 12
TZ = 256
PAY = CH + TZ + 16
STRIP = 128
STRIPS = PIX // STRIP
PIECES = ((0, 4), (4, 8))
AXES = ("segment", "slab")
SCALE = CH / PIX
F32 = jnp.float32
BF16 = jnp.bfloat16


def linear(x, y, z, core):
    return ((y % 2) * 2 + core) * 32 + (x % 4) * 8 + (y // 2) * 4 + z % 4


def devices():
    for x in range(4):
        for y in range(4):
            for z in range(4):
                for core in range(2):
                    yield x, y, z, core


def home(slab, batch, core):
    x, y_hi, z = slab // 8, slab // 4 % 2, slab % 4
    return linear(x, batch if y_hi == 0 else 3 - batch, z, core)


def batch_of(y):
    return y % 2 ^ y // 2


def main_pairs():
    return [
        (home(x * 8 + core * 4 + z, batch_of(y), core), linear(x, y, z, core))
        for x, y, z, core in devices()
        if core != y // 2
    ]


def side_pairs(shift):
    pairs = []
    for x, y, z, core in devices():
        slab = x * 8 + core * 4 + z + shift
        if 0 <= slab < 32:
            pairs.append((home(slab, batch_of(y), y // 2), linear(x, y, z, core)))
    return pairs


def torus_pairs(even, odd):
    pairs = []
    for x, y, z, core in devices():
        dx, dz = odd if (x + z) % 2 else even
        pairs.append((linear(x + dx, y, z + dz, core), linear(x, y, z, core)))
    return pairs


A1, B1, C1 = ((2, 0), (0, 2)), ((0, 1), (1, 0)), ((0, -1), (-1, 0))
NEAR = (
    (0, (1, 0), (0, 1)),
    (0, (-1, 0), (0, -1)),
    (1, (0, 1), (1, 0)),
    (1, (0, -1), (-1, 0)),
)
FAR = (
    (0, 0, (0, 1), (1, 0)),
    (1, 1, (0, -1), (-1, 0)),
    (2, 0, (1, 0), (0, 1)),
    (3, 1, (-1, 0), (0, -1)),
)


def block_table():
    table = np.zeros((16, 16), np.int32)
    for x in range(4):
        for z in range(4):

            def first(px, pz):
                odd = (px + pz) % 2
                out = [(px, pz)]
                for offsets in (A1, B1, C1):
                    dx, dz = offsets[odd]
                    out.append((px + dx, pz + dz))
                return out

            found = first(x, z)

            def second(px, pz, arrival):
                which, even, odd = NEAR[arrival]
                dx, dz = odd if (px + pz) % 2 else even
                source = first(px + dx, pz + dz)
                return source[:2] if which == 0 else source[2:]

            for arrival in range(4):
                found += second(x, z, arrival)
            for arrival, which, even, odd in FAR:
                dx, dz = odd if (x + z) % 2 else even
                found.append(second(x + dx, z + dz, arrival)[which])
            found = [(px % 4, pz % 4) for px, pz in found]
            assert len(set(found)) == 16
            table[x * 4 + z] = [px * 8 + pz for px, pz in found]
    return table


def ramp_matrix():
    distance = np.arange(CH)[:, None] - np.arange(CHP)[None, :]
    odd = distance % 2 != 0
    taps = np.where(odd, -4.0 / (math.pi**2 * np.where(odd, distance, 1) ** 2.0), 0.0)
    taps = np.where(distance == 0, 1.0, taps) * (np.arange(CHP) < CH)
    return jnp.asarray(taps.astype(np.float32).astype(BF16))


def packed(view):
    return jnp.concatenate([view[: CH // 2], view[CH // 2 :]], axis=1)


def unpacked(ref):
    return jnp.concatenate([ref[:, :ROWS], ref[:, ROWS:]], axis=0)


def column(line):
    return jnp.broadcast_to(line.reshape(1, CH), (8, CH)).T[:, :1]


def message_kernel(batch_ref, feet_hbm, raw_hbm, weight_hbm, own_ref, last_ref, first_ref, feet_ref, sem):
    batch = batch_ref[0]
    copies = [
        pltpu.make_async_copy(raw_hbm.at[batch], own_ref.at[pl.ds(0, CH)], sem.at[0]),
        pltpu.make_async_copy(weight_hbm.at[batch, 0], own_ref.at[pl.ds(CH, TZ)], sem.at[1]),
        pltpu.make_async_copy(feet_hbm, feet_ref, sem.at[2]),
    ]
    for copy in copies:
        copy.start()
    for copy in copies:
        copy.wait()
    row = lax.broadcasted_iota(jnp.int32, (16, COLS), 0)
    lane = lax.broadcasted_iota(jnp.int32, (16, COLS), 1)
    feet = jnp.full((16, COLS), -1.0, F32)
    for slot in range(FOOT):
        here = jnp.logical_and(row == 0, lane == slot)
        feet = jnp.where(here, feet_ref[batch, 0, slot].astype(F32), feet)
    own_ref[CH + TZ :, :] = feet.astype(BF16)
    raw = own_ref[:CH, :]
    last_ref[...] = packed(raw[:, ROWS:])
    first_ref[...] = packed(raw[:, :ROWS])


def pair_kernel(one_ref, two_ref, *refs):
    out_ref = refs[-1]
    out_ref[0] = one_ref[...]
    out_ref[1] = two_ref[...]


def pick_kernel(which, pair_ref, _, out_ref):
    out_ref[...] = pair_ref[which]


def prepare_kernel(_, channel_ref, view_ref, weight_ref, ramp_hbm, pick_ref, column_ref, ramp_ref, sem):
    copy = pltpu.make_async_copy(ramp_hbm, ramp_ref, sem)
    copy.start()
    sources = column(view_ref[...] * CHP + channel_ref[...])
    column_ref[...] = column(weight_ref[...])
    channel = lax.broadcasted_iota(jnp.int32, (CH, CHP), 1)
    for tap in range(3):
        pick = jnp.where(channel == sources - tap * CHP, 1.0, 0.0).astype(BF16)
        pick_ref[:, pl.ds(tap * CHP, CHP)] = pick
    copy.wait()


def filter_kernel(mine_ref, own_ref, other_ref, low_ref, high_ref, pick_ref, column_ref, ramp_ref, out_ref, x_ref, r_ref):
    keep = mine_ref[0] != 0
    both = jnp.where(keep, own_ref[...], other_ref[...])
    raw = both[:CH]
    low = jnp.concatenate([unpacked(low_ref), raw[:, :ROWS]], axis=1)
    high = jnp.concatenate([raw[:, ROWS:], unpacked(high_ref)], axis=1)
    for tap, part in enumerate((low, raw, high)):
        up = jnp.concatenate([part[1:], part[:1]], axis=0)
        rows = pl.ds(tap * CHP, CH)
        x_ref[rows, :COLS] = part
        x_ref[rows, COLS:] = up
        x_ref[pl.ds(tap * CHP + CH, CHP - CH), :] = jnp.zeros((CHP - CH, 2 * COLS), BF16)
    total = jnp.dot(pick_ref[...], x_ref[...], preferred_element_type=F32)
    weight = column_ref[...]
    r_ref[:CH, :] = ((1.0 - weight) * total[:, :COLS] + weight * total[:, COLS:]).astype(BF16)
    r_ref[CH:, :] = jnp.zeros((CHP - CH, COLS), BF16)
    out_ref[:CH, :] = jnp.dot(ramp_ref[...], r_ref[...], preferred_element_type=F32).astype(BF16)
    out_ref[CH:, :] = both[CH:]


def stage(base, names, tile_ref, f_ref, list_ref):
    lane = lax.broadcasted_iota(jnp.int32, (16, COLS), 1)
    row = lax.broadcasted_iota(jnp.int32, (16, COLS), 0)
    slots = []
    for block in names:
        feet = block[CH + TZ :, :].astype(F32)
        hit = jnp.logical_and(feet == tile_ref[0].astype(F32), row == 0)
        slots.append(jnp.sum(jnp.where(hit, lane + 1, 0).astype(F32)).astype(jnp.int32))
    list_ref[0] = 0
    for index, (slot, block) in enumerate(zip(slots, names)):

        @pl.when(slot > 0)
        def _():
            found = list_ref[0]
            f_ref[found] = block[: CH + TZ, :]
            list_ref[1 + 2 * found] = slot - 1
            list_ref[2 + 2 * found] = base + index
            list_ref[0] = found + 1


def weigh(f_ref, found, g_ref):
    col = lax.broadcasted_iota(jnp.int32, (TZ, COLS), 1)
    weight = f_ref[found, CH:, :]
    zero = jnp.zeros_like(weight)
    for view in range(2):
        part = jnp.where((col < ROWS) == (view == 0), weight, zero)
        g_ref[:, pl.ds(view * TZ, TZ)] = lax.dot_general(
            f_ref[found, :CH, :], part, (((1,), (1,)), ((), ())), preferred_element_type=F32
        ).astype(BF16)


def project(found, strips, list_ref, cos_ref, sin_ref, acc_ref, g_ref):
    slot, number = list_ref[1 + 2 * found], list_ref[2 + 2 * found]
    shift = (slot.astype(F32) - (FOOT - 1) / 2.0) * (PIX / (4.0 * FOOT))
    y_first = shift - (YR / 2.0 - 0.5)
    cos = [cos_ref[2 * number + view] * SCALE for view in range(2)]
    sin = [sin_ref[2 * number + view] * SCALE for view in range(2)]
    x_iota = lax.broadcasted_iota(jnp.int32, (STRIP, COLS), 0).astype(F32)
    c_iota = lax.broadcasted_iota(jnp.int32, (STRIP, COLS), 1).astype(F32)
    slope = [x_iota * cos[view] - c_iota for view in range(2)]
    reach = [
        jnp.minimum(0.0, (STRIP - 1) * cos[view]) + jnp.minimum(0.0, (YR - 1) * sin[view]) - 1.5
        for view in range(2)
    ]
    zero, one = jnp.zeros((), BF16), jnp.ones((), BF16)
    for place, strip in enumerate(strips):
        x_first = strip * STRIP - (PIX / 2.0 - 0.5)
        starts, parts = [], []
        for view in range(2):
            u = (CH - 1) / 2.0 + x_first * cos[view] + y_first * sin[view]
            low = jnp.clip(u + reach[view], 0.0, float(CH - COLS)).astype(jnp.int32)
            start = pl.multiple_of(lax.shift_left(lax.shift_right_logical(low, 4), 4), 16)
            offset = u - start.astype(F32)
            starts.append(start)
            rows = []
            for y in range(YR):
                away = jnp.abs((slope[view] + (offset + y * sin[view])).astype(BF16))
                rows.append(jnp.maximum(zero, one - away))
            parts.append(jnp.concatenate(rows, axis=0))
        mapped = jnp.concatenate(parts, axis=1)
        right = jnp.concatenate(
            [g_ref[pl.ds(starts[view], COLS), pl.ds(view * TZ, TZ)] for view in range(2)], axis=0
        )
        rows = pl.ds(place * (YR * STRIP), YR * STRIP)
        acc_ref[rows, :] += jnp.dot(mapped, right, preferred_element_type=F32)


def each_block(strips, list_ref, cos_ref, sin_ref, acc_ref, f_ref, g_ref, h_ref, done=None):
    count = list_ref[0]

    def step(found, now_ref, next_ref):
        weigh(f_ref, jnp.minimum(found + 1, count - 1), next_ref)
        project(found, strips, list_ref, cos_ref, sin_ref, acc_ref, now_ref)
        if done is not None:
            done(found, now_ref)

    @pl.when(count > 0)
    def _():
        weigh(f_ref, 0, g_ref)

    def two(pair, carry):
        step(2 * pair, g_ref, h_ref)

        @pl.when(2 * pair + 1 < count)
        def _():
            step(2 * pair + 1, h_ref, g_ref)

        return carry

    lax.fori_loop(0, (count + 1) // 2, two, 0)


def own_kernel(tile_ref, cos_ref, sin_ref, block_ref, acc_ref, g_ref, f_ref, list_ref):
    stage(0, [block_ref], tile_ref, f_ref, list_ref)
    acc_ref[...] = jnp.zeros_like(acc_ref)

    @pl.when(list_ref[0] > 0)
    def _():
        weigh(f_ref, 0, g_ref)
        project(0, range(STRIPS), list_ref, cos_ref, sin_ref, acc_ref, g_ref)


def first_kernel(tile_ref, cos_ref, sin_ref, b1, b2, b3, old_ref, acc_ref, g_ref, h_ref, f_ref, list_ref):
    stage(1, [b1, b2, b3], tile_ref, f_ref, list_ref)
    acc_ref[...] = old_ref[...]
    each_block(range(STRIPS), list_ref, cos_ref, sin_ref, acc_ref, f_ref, g_ref, h_ref)


def middle_kernel(tile_ref, cos_ref, sin_ref, p0, p1, p2, p3, old_ref, acc_ref, g_ref, h_ref, f_ref, list_ref):
    names = [pair.at[i] for pair in (p0, p1, p2, p3) for i in range(2)]
    stage(4, names, tile_ref, f_ref, list_ref)
    acc_ref[...] = old_ref[...]
    each_block(range(STRIPS), list_ref, cos_ref, sin_ref, acc_ref, f_ref, g_ref, h_ref)


def turn(core, acc_ref, send_ref, keep_ref):
    width = acc_ref.shape[0] // YR

    def one_strip(strip, carry):
        for y in range(YR):
            rows = pl.ds(pl.multiple_of(strip * (YR * STRIP) + y * STRIP, STRIP), STRIP)
            turned = acc_ref[rows, :].T
            cols = pl.ds(pl.multiple_of(strip * STRIP + y * width, STRIP), STRIP)
            keep_ref[:64, cols] = jnp.where(core == 0, turned[:64], turned[64:128])
            keep_ref[64:, cols] = jnp.where(core == 0, turned[128:192], turned[192:])
            send_ref[:64, cols] = jnp.where(core == 0, turned[64:128], turned[:64]).astype(BF16)
            send_ref[64:, cols] = jnp.where(core == 0, turned[192:], turned[128:192]).astype(BF16)
        return carry

    lax.fori_loop(0, width // STRIP, one_strip, 0)


def left_kernel(
    tile_ref, cos_ref, sin_ref, b0, b1, b2, b3, old_ref, send_ref, keep_ref, kept_ref, list_ref, acc_ref, g_ref, h_ref, f_ref
):
    stage(12, [b0, b1, b2, b3], tile_ref, f_ref, list_ref)
    acc_ref[...] = old_ref[: acc_ref.shape[0], :]

    def done(found, now_ref):
        kept_ref[found] = now_ref[...]

    each_block(range(*PIECES[0]), list_ref, cos_ref, sin_ref, acc_ref, f_ref, g_ref, h_ref, done)
    turn(tile_ref[1], acc_ref, send_ref, keep_ref)


def right_kernel(piece, tile_ref, cos_ref, sin_ref, list_ref, kept_ref, old_ref, send_ref, keep_ref, acc_ref):
    low, high = PIECES[piece]
    acc_ref[...] = old_ref[low * YR * STRIP : high * YR * STRIP, :]

    def one_block(found, carry):
        project(found, range(low, high), list_ref, cos_ref, sin_ref, acc_ref, kept_ref.at[found])
        return carry

    lax.fori_loop(0, list_ref[0], one_block, 0)
    turn(tile_ref[1], acc_ref, send_ref, keep_ref)


def half_kernel(chip_ref, keep_ref, got_ref, *refs):
    send_ref, rest_ref = refs[-2:]
    chip = chip_ref[0]
    mine = pl.ds(pl.multiple_of(chip * 64, 64), 64)
    theirs = pl.ds(pl.multiple_of((1 - chip) * 64, 64), 64)
    send_ref[...] = (keep_ref[theirs, :] + got_ref[theirs, :].astype(F32)).astype(BF16)
    rest_ref[...] = keep_ref[mine, :] + got_ref[mine, :].astype(F32)


def sum_kernel(piece, rest_ref, got_ref, *refs):
    out_ref, sum_ref, sem = refs[-3:]
    low, high = PIECES[piece]
    width = (high - low) * STRIP
    copies = []
    for y in range(YR):
        cols = pl.ds(y * width, width)
        sum_ref[:, cols] = rest_ref[:, cols] + got_ref[:, cols].astype(F32)
        place = out_ref.at[0, :, pl.ds(y * PIX + low * STRIP, width)]
        copies.append(pltpu.make_async_copy(sum_ref.at[:, cols], place, sem.at[y]))
    for copy in copies:
        copy.start()
    for copy in copies:
        copy.wait()


VMEM = pl.BlockSpec(memory_space=pltpu.VMEM)
SMEM = pl.BlockSpec(memory_space=pltpu.SMEM)
HBM = pl.BlockSpec(memory_space=pltpu.HBM)
LATER = pl.BlockSpec(memory_space=pl.ANY)


def stay(array):
    return pltpu.with_memory_space_constraint(array, pltpu.HBM)


def shape(dims, dtype):
    return jax.ShapeDtypeStruct(dims, dtype)


def cost(flops, moved):
    return pl.CostEstimate(flops=flops, bytes_accessed=moved, transcendentals=0)


LIMIT = 24 * 2**20
BLOCK_FLOPS = 2 * 4096 * 256 * 256 + 2 * CH * COLS * 512
PIXELS = YR * PIX


def shards(raw_views, tap_channel, tap_view, tap_weight, batch_view, footprint, plane_weight):
    segment = lax.axis_index("segment")
    slab = lax.axis_index("slab")
    chip, core = segment // 2, segment % 2
    x_pos, y_hi, z_pos = slab // 8, slab // 4 % 2, slab % 4
    batch = jnp.bitwise_xor(chip, y_hi)

    def call(kernel, out_shape, in_specs, *operands, scratch=(), work=(10**5, 10**6), limit=LIMIT):
        many = isinstance(out_shape, tuple)
        return pl.pallas_call(
            kernel,
            out_shape=out_shape,
            in_specs=in_specs,
            out_specs=tuple(SMEM if o.dtype == jnp.int32 else VMEM for o in out_shape) if many else VMEM,
            scratch_shapes=list(scratch),
            compiler_params=pltpu.CompilerParams(vmem_limit_bytes=limit),
            cost_estimate=cost(*work),
        )(*operands)

    own, last, first = call(
        message_kernel,
        (shape((PAY, COLS), BF16), shape((CH // 2, COLS), BF16), shape((CH // 2, COLS), BF16)),
        [SMEM, HBM, HBM, HBM],
        batch[None],
        stay(footprint),
        stay(raw_views),
        stay(plane_weight),
        scratch=[pltpu.SMEM((2, 1, FOOT), jnp.int32), pltpu.SemaphoreType.DMA((3,))],
    )
    other = lax.ppermute(own, AXES, main_pairs())
    low = lax.ppermute(last, AXES, side_pairs(-1))
    high = lax.ppermute(first, AXES, side_pairs(1))

    prepared = call(
        prepare_kernel,
        (shape((CH, 3 * CHP), BF16), shape((CH, 1), F32), shape((CH, CHP), BF16)),
        [LATER, VMEM, VMEM, VMEM, HBM],
        own,
        stay(tap_channel),
        stay(tap_view),
        stay(tap_weight),
        stay(ramp_matrix()),
        scratch=[pltpu.SemaphoreType.DMA],
        work=(10**6, 4 * 10**6),
    )
    payload = call(
        filter_kernel,
        shape((PAY, COLS), BF16),
        [SMEM] + [VMEM] * 7,
        (core == y_hi).astype(jnp.int32)[None],
        own,
        other,
        low,
        high,
        *prepared,
        scratch=[pltpu.VMEM((3 * CHP, 2 * COLS), BF16), pltpu.VMEM((CHP, COLS), BF16)],
        work=(4 * 10**9, 4 * 10**6),
    )
    payload, batch_view = lax.optimization_barrier((payload, batch_view))
    got_a = lax.ppermute(payload, AXES, torus_pairs(*A1))
    got_b = lax.ppermute(payload, AXES, torus_pairs(*B1))
    got_c = lax.ppermute(payload, AXES, torus_pairs(*C1))
    blocks = lax.dynamic_index_in_dim(jnp.asarray(block_table()), x_pos * 4 + z_pos, 0, keepdims=False)
    first_view = lax.dynamic_index_in_dim(batch_view, batch, 0, keepdims=False)
    views = jnp.arange(32, dtype=jnp.int32)
    angle = first_view + 2 * (jnp.repeat(blocks, 2) + core * 4) + views % 2
    theta = angle.astype(F32) * (2.0 * math.pi / VPT)
    cos, sin = jnp.cos(theta), jnp.sin(theta)
    tile = jnp.where(jnp.arange(2) == 0, slab, core).astype(jnp.int32)

    two = shape((2, PAY, COLS), BF16)
    accumulator = shape((PIXELS, TZ), F32)
    total = call(
        own_kernel, accumulator, [SMEM] * 3 + [VMEM],
        tile, cos, sin, payload,
        scratch=[pltpu.VMEM((CH, 2 * TZ), BF16), pltpu.VMEM((1, CH + TZ, COLS), BF16), pltpu.SMEM((3,), jnp.int32)],
        work=(BLOCK_FLOPS, 10**6),
    )
    pairs = (
        call(pair_kernel, two, [VMEM, VMEM], payload, got_a),
        call(pair_kernel, two, [VMEM, VMEM, LATER], got_b, got_c, total),
    )
    near = [lax.ppermute(pairs[which], AXES, torus_pairs(even, odd)) for which, even, odd in NEAR]

    def scratch(count, listed=True):
        weighed = [pltpu.VMEM((CH, 2 * TZ), BF16)] * (2 if count > 1 else 1)
        found = [pltpu.VMEM((count, CH + TZ, COLS), BF16)]
        return weighed + found + [pltpu.SMEM((1 + 2 * count,), jnp.int32)] * listed

    total = call(
        first_kernel, accumulator, [SMEM] * 3 + [VMEM] * 4,
        tile, cos, sin, got_a, got_b, got_c, total,
        scratch=scratch(3), work=(3 * BLOCK_FLOPS, 5 * 10**6),
    )
    far = []
    for arrival, which, even, odd in FAR:
        passed = call(
            functools.partial(pick_kernel, which), shape((PAY, COLS), BF16), [VMEM, LATER], near[arrival], total
        )
        far.append(lax.ppermute(passed, AXES, torus_pairs(even, odd)))
    total = call(
        middle_kernel, accumulator, [SMEM] * 3 + [VMEM] * 5,
        tile, cos, sin, *near, total,
        scratch=scratch(8), work=(8 * BLOCK_FLOPS, 10**7),
    )
    beside = [(s * 32 + t, (s ^ 1) * 32 + t) for s in range(4) for t in range(32)]
    across = [(s * 32 + t, (s ^ 2) * 32 + t) for s in range(4) for t in range(32)]
    ends, before = [], []
    for piece, (first_strip, last_strip) in enumerate(PIECES):
        pixels = (last_strip - first_strip) * STRIP * YR
        outputs = (shape((COLS, pixels), BF16), shape((COLS, pixels), F32))
        acc = [pltpu.VMEM((pixels, TZ), F32)]
        if piece == 0:
            send, keep, kept, slots = call(
                left_kernel,
                outputs + (shape((4, CH, 2 * TZ), BF16), shape((9,), jnp.int32)),
                [SMEM] * 3 + [VMEM] * 5,
                tile, cos, sin, *far, total,
                scratch=acc + scratch(4, False), work=(2 * BLOCK_FLOPS, 9 * 10**6),
            )
        else:
            send, keep = call(
                functools.partial(right_kernel, piece),
                outputs,
                [SMEM] * 4 + [VMEM] * 2,
                tile, cos, sin, slots, kept, total,
                scratch=acc, work=(BLOCK_FLOPS, 4 * 10**6),
            )
        swapped = lax.ppermute(send, AXES, beside)
        send, rest = call(
            half_kernel,
            (shape((64, pixels), BF16), shape((64, pixels), F32)),
            [SMEM, VMEM, VMEM] + [LATER] * len(before),
            chip[None], keep, swapped, *before,
        )
        before = [send]
        ends.append((rest, lax.ppermute(send, AXES, across)))
    image = None
    for piece, (rest, swapped) in enumerate(ends):
        held = [image] if piece else []
        image = pl.pallas_call(
            functools.partial(sum_kernel, piece),
            out_shape=shape((1, 64, PIXELS), F32),
            in_specs=[VMEM, VMEM] + [LATER] * len(held),
            out_specs=LATER,
            scratch_shapes=[pltpu.VMEM(rest.shape, F32), pltpu.SemaphoreType.DMA((YR,))],
            input_output_aliases={2: 0} if held else {},
            compiler_params=pltpu.CompilerParams(vmem_limit_bytes=LIMIT),
            cost_estimate=cost(10**5, 10**6),
        )(rest, swapped, *held)
    return image


def solution(mesh):
    return jax.shard_map(
        shards,
        mesh=mesh,
        in_specs=(
            P(None, None, "slab"),
            P(),
            P(),
            P(),
            P(),
            P(None, "slab", None),
            P(None, "slab", None, None),
        ),
        out_specs=P("slab", "segment", None),
        check_vma=False,
    )
```

```python
import functools
import math

import jax
import jax.numpy as jnp
import numpy as np
from jax import lax
from jax.experimental import pallas as pl
from jax.experimental.pallas import tpu as pltpu
from jax.sharding import PartitionSpec as P

CH = 736
CHP = 768
ROWS = 64
COLS = 128
PIX = 1024
YR = 4
VPT = 1152
FOOT = 12
TZ = 256
PAY = CH + TZ + 16
STRIP = 128
STRIPS = PIX // STRIP
NARROW = 64
NARROWS = PIX // NARROW
PIECES = ((0, 4), (4, 8))
AXES = ("segment", "slab")
SCALE = CH / PIX
F32 = jnp.float32
BF16 = jnp.bfloat16


def linear(x, y, z, core):
    return ((y % 2) * 2 + core) * 32 + (x % 4) * 8 + (y // 2) * 4 + z % 4


def devices():
    for x in range(4):
        for y in range(4):
            for z in range(4):
                for core in range(2):
                    yield x, y, z, core


def home(slab, batch, core):
    x, y_hi, z = slab // 8, slab // 4 % 2, slab % 4
    return linear(x, batch if y_hi == 0 else 3 - batch, z, core)


def batch_of(y):
    return y % 2 ^ y // 2


def main_pairs():
    return [
        (home(x * 8 + core * 4 + z, batch_of(y), core), linear(x, y, z, core))
        for x, y, z, core in devices()
        if core != y // 2
    ]


def side_pairs(shift):
    pairs = []
    for x, y, z, core in devices():
        slab = x * 8 + core * 4 + z + shift
        if 0 <= slab < 32:
            pairs.append((home(slab, batch_of(y), y // 2), linear(x, y, z, core)))
    return pairs


def torus_pairs(even, odd):
    pairs = []
    for x, y, z, core in devices():
        dx, dz = odd if (x + z) % 2 else even
        pairs.append((linear(x + dx, y, z + dz, core), linear(x, y, z, core)))
    return pairs


A1, B1, C1 = ((2, 0), (0, 2)), ((0, 1), (1, 0)), ((0, -1), (-1, 0))
NEAR = (
    (0, (1, 0), (0, 1)),
    (0, (-1, 0), (0, -1)),
    (1, (0, 1), (1, 0)),
    (1, (0, -1), (-1, 0)),
)
FAR = (
    (0, 0, (0, 1), (1, 0)),
    (1, 1, (0, -1), (-1, 0)),
    (2, 0, (1, 0), (0, 1)),
    (3, 1, (-1, 0), (0, -1)),
)


def block_table():
    table = np.zeros((16, 16), np.int32)
    for x in range(4):
        for z in range(4):

            def first(px, pz):
                odd = (px + pz) % 2
                out = [(px, pz)]
                for offsets in (A1, B1, C1):
                    dx, dz = offsets[odd]
                    out.append((px + dx, pz + dz))
                return out

            found = first(x, z)

            def second(px, pz, arrival):
                which, even, odd = NEAR[arrival]
                dx, dz = odd if (px + pz) % 2 else even
                source = first(px + dx, pz + dz)
                return source[:2] if which == 0 else source[2:]

            for arrival in range(4):
                found += second(x, z, arrival)
            for arrival, which, even, odd in FAR:
                dx, dz = odd if (x + z) % 2 else even
                found.append(second(x + dx, z + dz, arrival)[which])
            found = [(px % 4, pz % 4) for px, pz in found]
            assert len(set(found)) == 16
            table[x * 4 + z] = [px * 8 + pz for px, pz in found]
    return table


def ramp_matrix():
    distance = np.arange(CH)[:, None] - np.arange(CHP)[None, :]
    odd = distance % 2 != 0
    taps = np.where(odd, -4.0 / (math.pi**2 * np.where(odd, distance, 1) ** 2.0), 0.0)
    taps = np.where(distance == 0, 1.0, taps) * (np.arange(CHP) < CH)
    return jnp.asarray(taps.astype(np.float32).astype(BF16))


def packed(view):
    return jnp.concatenate([view[: CH // 2], view[CH // 2 :]], axis=1)


def unpacked(ref):
    return jnp.concatenate([ref[:, :ROWS], ref[:, ROWS:]], axis=0)


def column(line):
    return jnp.broadcast_to(line.reshape(1, CH), (8, CH)).T[:, :1]


def message_kernel(batch_ref, feet_hbm, raw_hbm, weight_hbm, own_ref, last_ref, first_ref, feet_ref, sem):
    batch = batch_ref[0]
    copies = [
        pltpu.make_async_copy(raw_hbm.at[batch], own_ref.at[pl.ds(0, CH)], sem.at[0]),
        pltpu.make_async_copy(weight_hbm.at[batch, 0], own_ref.at[pl.ds(CH, TZ)], sem.at[1]),
        pltpu.make_async_copy(feet_hbm, feet_ref, sem.at[2]),
    ]
    for copy in copies:
        copy.start()
    for copy in copies:
        copy.wait()
    row = lax.broadcasted_iota(jnp.int32, (16, COLS), 0)
    lane = lax.broadcasted_iota(jnp.int32, (16, COLS), 1)
    feet = jnp.full((16, COLS), -1.0, F32)
    for slot in range(FOOT):
        here = jnp.logical_and(row == 0, lane == slot)
        feet = jnp.where(here, feet_ref[batch, 0, slot].astype(F32), feet)
    own_ref[CH + TZ :, :] = feet.astype(BF16)
    raw = own_ref[:CH, :]
    last_ref[...] = packed(raw[:, ROWS:])
    first_ref[...] = packed(raw[:, :ROWS])


def pair_kernel(one_ref, two_ref, *refs):
    out_ref = refs[-1]
    out_ref[0] = one_ref[...]
    out_ref[1] = two_ref[...]


def pick_kernel(which, pair_ref, _, out_ref):
    out_ref[...] = pair_ref[which]


def prepare_kernel(_, channel_ref, view_ref, weight_ref, ramp_hbm, pick_ref, column_ref, ramp_ref, sem):
    copy = pltpu.make_async_copy(ramp_hbm, ramp_ref, sem)
    copy.start()
    sources = column(view_ref[...] * CHP + channel_ref[...])
    column_ref[...] = column(weight_ref[...])
    channel = lax.broadcasted_iota(jnp.int32, (CH, CHP), 1)
    for tap in range(3):
        pick = jnp.where(channel == sources - tap * CHP, 1.0, 0.0).astype(BF16)
        pick_ref[:, pl.ds(tap * CHP, CHP)] = pick
    copy.wait()


def filter_kernel(mine_ref, own_ref, other_ref, low_ref, high_ref, pick_ref, column_ref, ramp_ref, out_ref, x_ref, r_ref):
    keep = mine_ref[0] != 0
    both = jnp.where(keep, own_ref[...], other_ref[...])
    raw = both[:CH]
    low = jnp.concatenate([unpacked(low_ref), raw[:, :ROWS]], axis=1)
    high = jnp.concatenate([raw[:, ROWS:], unpacked(high_ref)], axis=1)
    for tap, part in enumerate((low, raw, high)):
        up = jnp.concatenate([part[1:], part[:1]], axis=0)
        rows = pl.ds(tap * CHP, CH)
        x_ref[rows, :COLS] = part
        x_ref[rows, COLS:] = up
        x_ref[pl.ds(tap * CHP + CH, CHP - CH), :] = jnp.zeros((CHP - CH, 2 * COLS), BF16)
    total = jnp.dot(pick_ref[...], x_ref[...], preferred_element_type=F32)
    weight = column_ref[...]
    r_ref[:CH, :] = ((1.0 - weight) * total[:, :COLS] + weight * total[:, COLS:]).astype(BF16)
    r_ref[CH:, :] = jnp.zeros((CHP - CH, COLS), BF16)
    out_ref[:CH, :] = jnp.dot(ramp_ref[...], r_ref[...], preferred_element_type=F32).astype(BF16)
    out_ref[CH:, :] = both[CH:]


def stage(base, names, tile_ref, f_ref, list_ref):
    lane = lax.broadcasted_iota(jnp.int32, (16, COLS), 1)
    row = lax.broadcasted_iota(jnp.int32, (16, COLS), 0)
    slots = []
    for block in names:
        feet = block[CH + TZ :, :].astype(F32)
        hit = jnp.logical_and(feet == tile_ref[0].astype(F32), row == 0)
        slots.append(jnp.sum(jnp.where(hit, lane + 1, 0).astype(F32)).astype(jnp.int32))
    list_ref[0] = 0
    for index, (slot, block) in enumerate(zip(slots, names)):

        @pl.when(slot > 0)
        def _():
            found = list_ref[0]
            f_ref[found] = block[: CH + TZ, :]
            list_ref[1 + 2 * found] = slot - 1
            list_ref[2 + 2 * found] = base + index
            list_ref[0] = found + 1


def weigh(f_ref, found, g_ref):
    col = lax.broadcasted_iota(jnp.int32, (TZ, COLS), 1)
    weight = f_ref[found, CH:, :]
    zero = jnp.zeros_like(weight)
    for view in range(2):
        part = jnp.where((col < ROWS) == (view == 0), weight, zero)
        g_ref[:, pl.ds(view * TZ, TZ)] = lax.dot_general(
            f_ref[found, :CH, :], part, (((1,), (1,)), ((), ())), preferred_element_type=F32
        ).astype(BF16)


def project(first, strips, list_ref, cos_ref, sin_ref, acc_ref, g_refs):
    count = list_ref[0]
    lane = lax.broadcasted_iota(jnp.int32, (NARROW, COLS), 1)
    early = lane < NARROW
    x_iota = lax.broadcasted_iota(jnp.int32, (NARROW, COLS), 0).astype(F32)
    c_iota = jnp.where(early, lane, lane - NARROW).astype(F32)
    early = early[:8]
    blocks = []
    for half in range(2):
        found = jnp.minimum(first + half, count - 1)
        slot, number = list_ref[1 + 2 * found], list_ref[2 + 2 * found]
        shift = (slot.astype(F32) - (FOOT - 1) / 2.0) * (PIX / (4.0 * FOOT))
        y_first = shift - (YR / 2.0 - 0.5)
        cos = [cos_ref[2 * number + view] * SCALE for view in range(2)]
        sin = [sin_ref[2 * number + view] * SCALE for view in range(2)]
        slope = x_iota * jnp.where(lane < NARROW, cos[0], cos[1]) - c_iota
        reach = [
            jnp.minimum(0.0, (NARROW - 1) * cos[view]) + jnp.minimum(0.0, (YR - 1) * sin[view]) - 0.01
            for view in range(2)
        ]
        absent = jnp.where(first + half < count, 0.0, 4096.0)
        blocks.append((y_first, cos, sin, slope, reach, absent))
    zero, one = jnp.zeros((), BF16), jnp.ones((), BF16)
    for place, strip in enumerate(strips):
        x_first = strip * NARROW - (PIX / 2.0 - 0.5)
        windows, parts = [], []
        for (y_first, cos, sin, slope, reach, absent), g_ref in zip(blocks, g_refs):
            offset = []
            for view in range(2):
                u = (CH - 1) / 2.0 + x_first * cos[view] + y_first * sin[view]
                low = jnp.clip(u + reach[view], 0.0, float(CH - NARROW)).astype(jnp.int32)
                start = pl.multiple_of(lax.shift_left(lax.shift_right_logical(low, 4), 4), 16)
                offset.append(u - start.astype(F32) + absent)
                windows.append(g_ref[pl.ds(start, NARROW), pl.ds(view * TZ, TZ)])
            rows = []
            for y in range(YR):
                move = jnp.where(early, offset[0] + y * sin[0], offset[1] + y * sin[1])
                away = jnp.abs((slope + jnp.concatenate([move] * (NARROW // 8), axis=0)).astype(BF16))
                rows.append(jnp.maximum(zero, one - away))
            parts.append(jnp.concatenate(rows, axis=0))
        term = jnp.dot(
            jnp.concatenate(parts, axis=1),
            jnp.concatenate(windows, axis=0),
            preferred_element_type=F32,
        )
        for y in range(YR):
            row = place // 2 * (YR * STRIP) + y * STRIP + place % 2 * NARROW
            acc_ref[pl.ds(row, NARROW), :] += term[y * NARROW : (y + 1) * NARROW]


def each_pair(strips, fill, list_ref, cos_ref, sin_ref, acc_ref, f_ref, now, later, done=None):
    count = list_ref[0]

    def weigh_pair(first, g_refs):
        for half in range(2):
            weigh(f_ref, jnp.minimum(first + half, count - 1), g_refs[half])

    def step(first, now_refs, next_refs):
        weigh_pair(first + 2, next_refs)
        project(first, strips, list_ref, cos_ref, sin_ref, acc_ref, now_refs)
        if done is not None:
            done(first, now_refs)

    @pl.when(count > 0)
    def _():
        weigh_pair(0, now)
        fill()

    @pl.when(count == 0)
    def _():
        fill()

    def four(index, carry):
        step(4 * index, now, later)

        @pl.when(4 * index + 2 < count)
        def _():
            step(4 * index + 2, later, now)

        return carry

    lax.fori_loop(0, (count + 3) // 4, four, 0)


def own_kernel(tile_ref, cos_ref, sin_ref, block_ref, acc_ref, g_ref, f_ref, list_ref):
    stage(0, [block_ref], tile_ref, f_ref, list_ref)

    def fill():
        acc_ref[...] = jnp.zeros_like(acc_ref)

    @pl.when(list_ref[0] > 0)
    def _():
        weigh(f_ref, 0, g_ref)
        fill()
        project(0, range(NARROWS), list_ref, cos_ref, sin_ref, acc_ref, (g_ref, g_ref))

    @pl.when(list_ref[0] == 0)
    def _():
        fill()


def later_kernel(base, size, tile_ref, cos_ref, sin_ref, *refs):
    names = []
    for ref in refs[:size]:
        names += [ref] if len(ref.shape) == 2 else [ref.at[0], ref.at[1]]
    old_ref, acc_ref, g0, g1, h0, h1, f_ref, list_ref = refs[size:]
    stage(base, names, tile_ref, f_ref, list_ref)

    def fill():
        acc_ref[...] = old_ref[...]

    each_pair(range(NARROWS), fill, list_ref, cos_ref, sin_ref, acc_ref, f_ref, (g0, g1), (h0, h1))


def turn(core, acc_ref, send_ref, keep_ref):
    width = acc_ref.shape[0] // YR

    def one_strip(strip, carry):
        for y in range(YR):
            rows = pl.ds(pl.multiple_of(strip * (YR * STRIP) + y * STRIP, STRIP), STRIP)
            turned = acc_ref[rows, :].T
            cols = pl.ds(pl.multiple_of(strip * STRIP + y * width, STRIP), STRIP)
            keep_ref[:64, cols] = jnp.where(core == 0, turned[:64], turned[64:128])
            keep_ref[64:, cols] = jnp.where(core == 0, turned[128:192], turned[192:])
            send_ref[:64, cols] = jnp.where(core == 0, turned[64:128], turned[:64]).astype(BF16)
            send_ref[64:, cols] = jnp.where(core == 0, turned[192:], turned[128:192]).astype(BF16)
        return carry

    lax.fori_loop(0, width // STRIP, one_strip, 0)


def left_kernel(tile_ref, cos_ref, sin_ref, *refs):
    old_ref, send_ref, keep_ref, kept_ref, list_ref, acc_ref, g0, g1, h0, h1, f_ref = refs[4:]
    stage(12, refs[:4], tile_ref, f_ref, list_ref)

    def fill():
        acc_ref[...] = old_ref[: acc_ref.shape[0], :]

    def done(first, now_refs):
        for half in range(2):
            kept_ref[first + half] = now_refs[half][...]

    strips = range(2 * PIECES[0][0], 2 * PIECES[0][1])
    each_pair(strips, fill, list_ref, cos_ref, sin_ref, acc_ref, f_ref, (g0, g1), (h0, h1), done)
    turn(tile_ref[1], acc_ref, send_ref, keep_ref)


def right_kernel(piece, tile_ref, cos_ref, sin_ref, list_ref, kept_ref, old_ref, send_ref, keep_ref, acc_ref):
    low, high = PIECES[piece]
    acc_ref[...] = old_ref[low * YR * STRIP : high * YR * STRIP, :]

    def one_pair(pair, carry):
        refs = kept_ref.at[2 * pair], kept_ref.at[2 * pair + 1]
        project(2 * pair, range(2 * low, 2 * high), list_ref, cos_ref, sin_ref, acc_ref, refs)
        return carry

    lax.fori_loop(0, (list_ref[0] + 1) // 2, one_pair, 0)
    turn(tile_ref[1], acc_ref, send_ref, keep_ref)


def half_kernel(chip_ref, keep_ref, got_ref, *refs):
    send_ref, rest_ref = refs[-2:]
    chip = chip_ref[0]
    mine = pl.ds(pl.multiple_of(chip * 64, 64), 64)
    theirs = pl.ds(pl.multiple_of((1 - chip) * 64, 64), 64)
    send_ref[...] = (keep_ref[theirs, :] + got_ref[theirs, :].astype(F32)).astype(BF16)
    rest_ref[...] = keep_ref[mine, :] + got_ref[mine, :].astype(F32)


def sum_kernel(piece, rest_ref, got_ref, *refs):
    out_ref, sum_ref, sem = refs[-3:]
    low, high = PIECES[piece]
    width = (high - low) * STRIP
    copies = []
    for y in range(YR):
        cols = pl.ds(y * width, width)
        sum_ref[:, cols] = rest_ref[:, cols] + got_ref[:, cols].astype(F32)
        place = out_ref.at[0, :, pl.ds(y * PIX + low * STRIP, width)]
        copies.append(pltpu.make_async_copy(sum_ref.at[:, cols], place, sem.at[y]))
    for copy in copies:
        copy.start()
    for copy in copies:
        copy.wait()


VMEM = pl.BlockSpec(memory_space=pltpu.VMEM)
SMEM = pl.BlockSpec(memory_space=pltpu.SMEM)
HBM = pl.BlockSpec(memory_space=pltpu.HBM)
LATER = pl.BlockSpec(memory_space=pl.ANY)


def stay(array):
    return pltpu.with_memory_space_constraint(array, pltpu.HBM)


def shape(dims, dtype):
    return jax.ShapeDtypeStruct(dims, dtype)


def cost(flops, moved):
    return pl.CostEstimate(flops=flops, bytes_accessed=moved, transcendentals=0)


LIMIT = 24 * 2**20
BLOCK_FLOPS = 2 * 4096 * 256 * 256 + 2 * CH * COLS * 512
PIXELS = YR * PIX


def shards(raw_views, tap_channel, tap_view, tap_weight, batch_view, footprint, plane_weight):
    segment = lax.axis_index("segment")
    slab = lax.axis_index("slab")
    chip, core = segment // 2, segment % 2
    x_pos, y_hi, z_pos = slab // 8, slab // 4 % 2, slab % 4
    batch = jnp.bitwise_xor(chip, y_hi)

    def call(kernel, out_shape, in_specs, *operands, scratch=(), work=(10**5, 10**6), limit=LIMIT):
        many = isinstance(out_shape, tuple)
        return pl.pallas_call(
            kernel,
            out_shape=out_shape,
            in_specs=in_specs,
            out_specs=tuple(SMEM if o.dtype == jnp.int32 else VMEM for o in out_shape) if many else VMEM,
            scratch_shapes=list(scratch),
            compiler_params=pltpu.CompilerParams(vmem_limit_bytes=limit),
            cost_estimate=cost(*work),
        )(*operands)

    own, last, first = call(
        message_kernel,
        (shape((PAY, COLS), BF16), shape((CH // 2, COLS), BF16), shape((CH // 2, COLS), BF16)),
        [SMEM, HBM, HBM, HBM],
        batch[None],
        stay(footprint),
        stay(raw_views),
        stay(plane_weight),
        scratch=[pltpu.SMEM((2, 1, FOOT), jnp.int32), pltpu.SemaphoreType.DMA((3,))],
    )
    other = lax.ppermute(own, AXES, main_pairs())
    low = lax.ppermute(last, AXES, side_pairs(-1))
    high = lax.ppermute(first, AXES, side_pairs(1))

    prepared = call(
        prepare_kernel,
        (shape((CH, 3 * CHP), BF16), shape((CH, 1), F32), shape((CH, CHP), BF16)),
        [LATER, VMEM, VMEM, VMEM, HBM],
        own,
        stay(tap_channel),
        stay(tap_view),
        stay(tap_weight),
        stay(ramp_matrix()),
        scratch=[pltpu.SemaphoreType.DMA],
        work=(10**6, 4 * 10**6),
    )
    payload = call(
        filter_kernel,
        shape((PAY, COLS), BF16),
        [SMEM] + [VMEM] * 7,
        (core == y_hi).astype(jnp.int32)[None],
        own,
        other,
        low,
        high,
        *prepared,
        scratch=[pltpu.VMEM((3 * CHP, 2 * COLS), BF16), pltpu.VMEM((CHP, COLS), BF16)],
        work=(4 * 10**9, 4 * 10**6),
    )
    payload, batch_view = lax.optimization_barrier((payload, batch_view))
    got_a = lax.ppermute(payload, AXES, torus_pairs(*A1))
    got_b = lax.ppermute(payload, AXES, torus_pairs(*B1))
    got_c = lax.ppermute(payload, AXES, torus_pairs(*C1))
    blocks = lax.dynamic_index_in_dim(jnp.asarray(block_table()), x_pos * 4 + z_pos, 0, keepdims=False)
    first_view = lax.dynamic_index_in_dim(batch_view, batch, 0, keepdims=False)
    views = jnp.arange(32, dtype=jnp.int32)
    angle = first_view + 2 * (jnp.repeat(blocks, 2) + core * 4) + views % 2
    theta = angle.astype(F32) * (2.0 * math.pi / VPT)
    cos, sin = jnp.cos(theta), jnp.sin(theta)
    tile = jnp.where(jnp.arange(2) == 0, slab, core).astype(jnp.int32)

    two = shape((2, PAY, COLS), BF16)
    accumulator = shape((PIXELS, TZ), F32)
    total = call(
        own_kernel, accumulator, [SMEM] * 3 + [VMEM],
        tile, cos, sin, payload,
        scratch=[pltpu.VMEM((CH, 2 * TZ), BF16), pltpu.VMEM((1, CH + TZ, COLS), BF16), pltpu.SMEM((3,), jnp.int32)],
        work=(BLOCK_FLOPS, 10**6),
    )
    pairs = (
        call(pair_kernel, two, [VMEM, VMEM], payload, got_a),
        call(pair_kernel, two, [VMEM, VMEM, LATER], got_b, got_c, total),
    )
    near = [lax.ppermute(pairs[which], AXES, torus_pairs(even, odd)) for which, even, odd in NEAR]

    def scratch(count, listed=True):
        weighed = [pltpu.VMEM((CH, 2 * TZ), BF16)] * 4
        found = [pltpu.VMEM((count, CH + TZ, COLS), BF16)]
        return weighed + found + [pltpu.SMEM((1 + 2 * count,), jnp.int32)] * listed

    total = call(
        functools.partial(later_kernel, 1, 3), accumulator, [SMEM] * 3 + [VMEM] * 4,
        tile, cos, sin, got_a, got_b, got_c, total,
        scratch=scratch(3), work=(3 * BLOCK_FLOPS, 5 * 10**6),
    )
    far = []
    for arrival, which, even, odd in FAR:
        passed = call(
            functools.partial(pick_kernel, which), shape((PAY, COLS), BF16), [VMEM, LATER], near[arrival], total
        )
        far.append(lax.ppermute(passed, AXES, torus_pairs(even, odd)))
    total = call(
        functools.partial(later_kernel, 4, 4), accumulator, [SMEM] * 3 + [VMEM] * 5,
        tile, cos, sin, *near, total,
        scratch=scratch(8), work=(8 * BLOCK_FLOPS, 10**7),
    )
    beside = [(s * 32 + t, (s ^ 1) * 32 + t) for s in range(4) for t in range(32)]
    across = [(s * 32 + t, (s ^ 2) * 32 + t) for s in range(4) for t in range(32)]
    ends, before = [], []
    for piece, (first_strip, last_strip) in enumerate(PIECES):
        pixels = (last_strip - first_strip) * STRIP * YR
        outputs = (shape((COLS, pixels), BF16), shape((COLS, pixels), F32))
        acc = [pltpu.VMEM((pixels, TZ), F32)]
        if piece == 0:
            send, keep, kept, slots = call(
                left_kernel,
                outputs + (shape((4, CH, 2 * TZ), BF16), shape((9,), jnp.int32)),
                [SMEM] * 3 + [VMEM] * 5,
                tile, cos, sin, *far, total,
                scratch=acc + scratch(4, False), work=(2 * BLOCK_FLOPS, 9 * 10**6),
            )
        else:
            send, keep = call(
                functools.partial(right_kernel, piece),
                outputs,
                [SMEM] * 4 + [VMEM] * 2,
                tile, cos, sin, slots, kept, total,
                scratch=acc, work=(BLOCK_FLOPS, 4 * 10**6),
            )
        swapped = lax.ppermute(send, AXES, beside)
        send, rest = call(
            half_kernel,
            (shape((64, pixels), BF16), shape((64, pixels), F32)),
            [SMEM, VMEM, VMEM] + [LATER] * len(before),
            chip[None], keep, swapped, *before,
        )
        before = [send]
        ends.append((rest, lax.ppermute(send, AXES, across)))
    image = None
    for piece, (rest, swapped) in enumerate(ends):
        held = [image] if piece else []
        image = pl.pallas_call(
            functools.partial(sum_kernel, piece),
            out_shape=shape((1, 64, PIXELS), F32),
            in_specs=[VMEM, VMEM] + [LATER] * len(held),
            out_specs=LATER,
            scratch_shapes=[pltpu.VMEM(rest.shape, F32), pltpu.SemaphoreType.DMA((YR,))],
            input_output_aliases={2: 0} if held else {},
            compiler_params=pltpu.CompilerParams(vmem_limit_bytes=LIMIT),
            cost_estimate=cost(10**5, 10**6),
        )(rest, swapped, *held)
    return image


def solution(mesh):
    return jax.shard_map(
        shards,
        mesh=mesh,
        in_specs=(
            P(None, None, "slab"),
            P(),
            P(),
            P(),
            P(),
            P(None, "slab", None),
            P(None, "slab", None, None),
        ),
        out_specs=P("slab", "segment", None),
        check_vma=False,
    )
```

```python
import functools
import math

import jax
import jax.numpy as jnp
import numpy as np
from jax import lax
from jax.experimental import pallas as pl
from jax.experimental.pallas import tpu as pltpu
from jax.sharding import PartitionSpec as P

CH = 736
CHP = 768
ROWS = 64
COLS = 128
PIX = 1024
YR = 4
VPT = 1152
FOOT = 12
TZ = 256
PAY = CH + TZ + 16
STRIP = 128
STRIPS = PIX // STRIP
NARROW = 64
NARROWS = PIX // NARROW
PIECES = ((0, 4), (4, 8))
AXES = ("segment", "slab")
SCALE = CH / PIX
F32 = jnp.float32
BF16 = jnp.bfloat16


def linear(x, y, z, core):
    return ((y % 2) * 2 + core) * 32 + (x % 4) * 8 + (y // 2) * 4 + z % 4


def devices():
    for x in range(4):
        for y in range(4):
            for z in range(4):
                for core in range(2):
                    yield x, y, z, core


def home(slab, batch, core):
    x, y_hi, z = slab // 8, slab // 4 % 2, slab % 4
    return linear(x, batch if y_hi == 0 else 3 - batch, z, core)


def batch_of(y):
    return y % 2 ^ y // 2


def main_pairs():
    return [
        (home(x * 8 + core * 4 + z, batch_of(y), core), linear(x, y, z, core))
        for x, y, z, core in devices()
        if core != y // 2
    ]


def side_pairs(shift):
    pairs = []
    for x, y, z, core in devices():
        slab = x * 8 + core * 4 + z + shift
        if 0 <= slab < 32:
            pairs.append((home(slab, batch_of(y), y // 2), linear(x, y, z, core)))
    return pairs


def torus_pairs(even, odd):
    pairs = []
    for x, y, z, core in devices():
        dx, dz = odd if (x + z) % 2 else even
        pairs.append((linear(x + dx, y, z + dz, core), linear(x, y, z, core)))
    return pairs


A1, B1, C1 = ((2, 0), (0, 2)), ((0, 1), (1, 0)), ((0, -1), (-1, 0))
NEAR = (
    (0, (1, 0), (0, 1)),
    (0, (-1, 0), (0, -1)),
    (1, (0, 1), (1, 0)),
    (1, (0, -1), (-1, 0)),
)
FAR = (
    (0, 0, (0, 1), (1, 0)),
    (1, 1, (0, -1), (-1, 0)),
    (2, 0, (1, 0), (0, 1)),
    (3, 1, (-1, 0), (0, -1)),
)


def block_table():
    table = np.zeros((16, 16), np.int32)
    for x in range(4):
        for z in range(4):

            def first(px, pz):
                odd = (px + pz) % 2
                out = [(px, pz)]
                for offsets in (A1, B1, C1):
                    dx, dz = offsets[odd]
                    out.append((px + dx, pz + dz))
                return out

            found = first(x, z)

            def second(px, pz, arrival):
                which, even, odd = NEAR[arrival]
                dx, dz = odd if (px + pz) % 2 else even
                source = first(px + dx, pz + dz)
                return source[:2] if which == 0 else source[2:]

            for arrival in range(4):
                found += second(x, z, arrival)
            for arrival, which, even, odd in FAR:
                dx, dz = odd if (x + z) % 2 else even
                found.append(second(x + dx, z + dz, arrival)[which])
            found = [(px % 4, pz % 4) for px, pz in found]
            assert len(set(found)) == 16
            table[x * 4 + z] = [px * 8 + pz for px, pz in found]
    return table


def ramp_matrix():
    distance = np.arange(CH)[:, None] - np.arange(CHP)[None, :]
    odd = distance % 2 != 0
    taps = np.where(odd, -4.0 / (math.pi**2 * np.where(odd, distance, 1) ** 2.0), 0.0)
    taps = np.where(distance == 0, 1.0, taps) * (np.arange(CHP) < CH)
    return jnp.asarray(taps.astype(np.float32).astype(BF16))


def packed(view):
    return jnp.concatenate([view[: CH // 2], view[CH // 2 :]], axis=1)


def unpacked(ref):
    return jnp.concatenate([ref[:, :ROWS], ref[:, ROWS:]], axis=0)


def column(line):
    return jnp.broadcast_to(line.reshape(1, CH), (8, CH)).T[:, :1]


def message_kernel(batch_ref, feet_hbm, raw_hbm, weight_hbm, own_ref, last_ref, first_ref, feet_ref, flat_ref, sem):
    batch = batch_ref[0]
    copies = [
        pltpu.make_async_copy(raw_hbm.at[batch], own_ref.at[pl.ds(0, CH)], sem.at[0]),
        pltpu.make_async_copy(weight_hbm.at[batch, 0], flat_ref, sem.at[1]),
        pltpu.make_async_copy(feet_hbm, feet_ref, sem.at[2]),
    ]
    for copy in copies:
        copy.start()
    for copy in copies:
        copy.wait()
    row = lax.broadcasted_iota(jnp.int32, (16, COLS), 0)
    lane = lax.broadcasted_iota(jnp.int32, (16, COLS), 1)
    feet = jnp.full((16, COLS), -1.0, F32)
    for slot in range(FOOT):
        here = jnp.logical_and(row == 0, lane == slot)
        feet = jnp.where(here, feet_ref[batch, 0, slot].astype(F32), feet)
    own_ref[CH + TZ :, :] = feet.astype(BF16)
    own_ref[CH : CH + COLS, :] = flat_ref[:COLS, :].astype(F32).T.astype(BF16)
    own_ref[CH + COLS : CH + TZ, :] = flat_ref[COLS:, :].astype(F32).T.astype(BF16)
    raw = own_ref[:CH, :]
    last_ref[...] = packed(raw[:, ROWS:])
    first_ref[...] = packed(raw[:, :ROWS])


def pair_kernel(one_ref, two_ref, *refs):
    out_ref = refs[-1]
    out_ref[0] = one_ref[...]
    out_ref[1] = two_ref[...]


def pick_kernel(which, pair_ref, _, out_ref):
    out_ref[...] = pair_ref[which]


def prepare_kernel(_, channel_ref, view_ref, weight_ref, ramp_hbm, pick_ref, column_ref, ramp_ref, sem):
    copy = pltpu.make_async_copy(ramp_hbm, ramp_ref, sem)
    copy.start()
    sources = column(view_ref[...] * CHP + channel_ref[...])
    column_ref[...] = column(weight_ref[...])
    channel = lax.broadcasted_iota(jnp.int32, (CH, CHP), 1)
    for tap in range(3):
        pick = jnp.where(channel == sources - tap * CHP, 1.0, 0.0).astype(BF16)
        pick_ref[:, pl.ds(tap * CHP, CHP)] = pick
    copy.wait()


def filter_kernel(mine_ref, own_ref, other_ref, low_ref, high_ref, pick_ref, column_ref, ramp_ref, out_ref, x_ref, r_ref):
    keep = mine_ref[0] != 0
    both = jnp.where(keep, own_ref[...], other_ref[...])
    raw = both[:CH]
    low = jnp.concatenate([unpacked(low_ref), raw[:, :ROWS]], axis=1)
    high = jnp.concatenate([raw[:, ROWS:], unpacked(high_ref)], axis=1)
    for tap, part in enumerate((low, raw, high)):
        up = jnp.concatenate([part[1:], part[:1]], axis=0)
        rows = pl.ds(tap * CHP, CH)
        x_ref[rows, :COLS] = part
        x_ref[rows, COLS:] = up
        x_ref[pl.ds(tap * CHP + CH, CHP - CH), :] = jnp.zeros((CHP - CH, 2 * COLS), BF16)
    total = jnp.dot(pick_ref[...], x_ref[...], preferred_element_type=F32)
    weight = column_ref[...]
    r_ref[:CH, :] = ((1.0 - weight) * total[:, :COLS] + weight * total[:, COLS:]).astype(BF16)
    r_ref[CH:, :] = jnp.zeros((CHP - CH, COLS), BF16)
    out_ref[:CH, :] = jnp.dot(ramp_ref[...], r_ref[...], preferred_element_type=F32).astype(BF16)
    out_ref[CH:, :] = both[CH:]


def stage(base, names, tile_ref, f_ref, list_ref):
    lane = lax.broadcasted_iota(jnp.int32, (16, COLS), 1)
    row = lax.broadcasted_iota(jnp.int32, (16, COLS), 0)
    slots = []
    for block in names:
        feet = block[CH + TZ :, :].astype(F32)
        hit = jnp.logical_and(feet == tile_ref[0].astype(F32), row == 0)
        slots.append(jnp.sum(jnp.where(hit, lane + 1, 0).astype(F32)).astype(jnp.int32))
    list_ref[0] = 0
    for index, (slot, block) in enumerate(zip(slots, names)):

        @pl.when(slot > 0)
        def _():
            found = list_ref[0]
            f_ref[found] = block[: CH + TZ, :]
            list_ref[1 + 2 * found] = slot - 1
            list_ref[2 + 2 * found] = base + index
            list_ref[0] = found + 1


def weigh(f_ref, found, g_ref):
    lane = lax.broadcasted_iota(jnp.int32, (CH, COLS), 1)
    values = f_ref[found, :CH, :]
    weight = jnp.concatenate([f_ref[found, CH : CH + COLS, :], f_ref[found, CH + COLS :, :]], axis=1)
    zero = jnp.zeros_like(values)
    for view in range(2):
        part = jnp.where((lane < ROWS) == (view == 0), values, zero)
        g_ref[:, pl.ds(view * TZ, TZ)] = jnp.dot(part, weight, preferred_element_type=F32).astype(BF16)


def project(first, strips, list_ref, cos_ref, sin_ref, acc_ref, g_refs):
    count = list_ref[0]
    lane = lax.broadcasted_iota(jnp.int32, (NARROW, COLS), 1)
    early = lane < NARROW
    x_iota = lax.broadcasted_iota(jnp.int32, (NARROW, COLS), 0).astype(F32)
    c_iota = jnp.where(early, lane, lane - NARROW).astype(F32)
    early = early[:8]
    blocks = []
    for half in range(2):
        found = jnp.minimum(first + half, count - 1)
        slot, number = list_ref[1 + 2 * found], list_ref[2 + 2 * found]
        shift = (slot.astype(F32) - (FOOT - 1) / 2.0) * (PIX / (4.0 * FOOT))
        y_first = shift - (YR / 2.0 - 0.5)
        cos = [cos_ref[2 * number + view] * SCALE for view in range(2)]
        sin = [sin_ref[2 * number + view] * SCALE for view in range(2)]
        slope = x_iota * jnp.where(lane < NARROW, cos[0], cos[1]) - c_iota
        reach = [
            jnp.minimum(0.0, (NARROW - 1) * cos[view]) + jnp.minimum(0.0, (YR - 1) * sin[view]) - 0.01
            for view in range(2)
        ]
        absent = jnp.where(first + half < count, 0.0, 4096.0)
        blocks.append((y_first, cos, sin, slope, reach, absent))
    zero, one = jnp.zeros((), BF16), jnp.ones((), BF16)
    for place, strip in enumerate(strips):
        x_first = strip * NARROW - (PIX / 2.0 - 0.5)
        windows, parts = [], []
        for (y_first, cos, sin, slope, reach, absent), g_ref in zip(blocks, g_refs):
            offset = []
            for view in range(2):
                u = (CH - 1) / 2.0 + x_first * cos[view] + y_first * sin[view]
                low = jnp.clip(u + reach[view], 0.0, float(CH - NARROW)).astype(jnp.int32)
                start = pl.multiple_of(lax.shift_left(lax.shift_right_logical(low, 4), 4), 16)
                offset.append(u - start.astype(F32) + absent)
                windows.append(g_ref[pl.ds(start, NARROW), pl.ds(view * TZ, TZ)])
            rows = []
            for y in range(YR):
                move = jnp.where(early, offset[0] + y * sin[0], offset[1] + y * sin[1])
                away = jnp.abs((slope + jnp.concatenate([move] * (NARROW // 8), axis=0)).astype(BF16))
                rows.append(jnp.maximum(zero, one - away))
            parts.append(jnp.concatenate(rows, axis=0))
        term = jnp.dot(
            jnp.concatenate(parts, axis=1),
            jnp.concatenate(windows, axis=0),
            preferred_element_type=F32,
        )
        for y in range(YR):
            row = place // 2 * (YR * STRIP) + y * STRIP + place % 2 * NARROW
            acc_ref[pl.ds(row, NARROW), :] += term[y * NARROW : (y + 1) * NARROW]


def each_pair(strips, fill, list_ref, cos_ref, sin_ref, acc_ref, f_ref, now, later, done=None):
    count = list_ref[0]

    def weigh_pair(first, g_refs):
        for half in range(2):
            weigh(f_ref, jnp.minimum(first + half, count - 1), g_refs[half])

    def step(first, now_refs, next_refs):
        weigh_pair(first + 2, next_refs)
        project(first, strips, list_ref, cos_ref, sin_ref, acc_ref, now_refs)
        if done is not None:
            done(first, now_refs)

    @pl.when(count > 0)
    def _():
        weigh_pair(0, now)
        fill()

    @pl.when(count == 0)
    def _():
        fill()

    def four(index, carry):
        step(4 * index, now, later)

        @pl.when(4 * index + 2 < count)
        def _():
            step(4 * index + 2, later, now)

        return carry

    lax.fori_loop(0, (count + 3) // 4, four, 0)


def own_kernel(tile_ref, cos_ref, sin_ref, block_ref, acc_ref, g_ref, f_ref, list_ref):
    stage(0, [block_ref], tile_ref, f_ref, list_ref)

    def fill():
        acc_ref[...] = jnp.zeros_like(acc_ref)

    @pl.when(list_ref[0] > 0)
    def _():
        weigh(f_ref, 0, g_ref)
        fill()
        project(0, range(NARROWS), list_ref, cos_ref, sin_ref, acc_ref, (g_ref, g_ref))

    @pl.when(list_ref[0] == 0)
    def _():
        fill()


def later_kernel(base, size, tile_ref, cos_ref, sin_ref, *refs):
    names = []
    for ref in refs[:size]:
        names += [ref] if len(ref.shape) == 2 else [ref.at[0], ref.at[1]]
    old_ref, acc_ref, g0, g1, h0, h1, f_ref, list_ref = refs[size:]
    stage(base, names, tile_ref, f_ref, list_ref)

    def fill():
        acc_ref[...] = old_ref[...]

    each_pair(range(NARROWS), fill, list_ref, cos_ref, sin_ref, acc_ref, f_ref, (g0, g1), (h0, h1))


def turn(core, acc_ref, send_ref, keep_ref):
    width = acc_ref.shape[0] // YR

    def one_strip(strip, carry):
        for y in range(YR):
            rows = pl.ds(pl.multiple_of(strip * (YR * STRIP) + y * STRIP, STRIP), STRIP)
            turned = acc_ref[rows, :].T
            cols = pl.ds(pl.multiple_of(strip * STRIP + y * width, STRIP), STRIP)
            keep_ref[:64, cols] = jnp.where(core == 0, turned[:64], turned[64:128])
            keep_ref[64:, cols] = jnp.where(core == 0, turned[128:192], turned[192:])
            send_ref[:64, cols] = jnp.where(core == 0, turned[64:128], turned[:64]).astype(BF16)
            send_ref[64:, cols] = jnp.where(core == 0, turned[192:], turned[128:192]).astype(BF16)
        return carry

    lax.fori_loop(0, width // STRIP, one_strip, 0)


def left_kernel(tile_ref, cos_ref, sin_ref, *refs):
    old_ref, send_ref, keep_ref, kept_ref, list_ref, acc_ref, g0, g1, h0, h1, f_ref = refs[4:]
    stage(12, refs[:4], tile_ref, f_ref, list_ref)

    def fill():
        acc_ref[...] = old_ref[: acc_ref.shape[0], :]

    def done(first, now_refs):
        for half in range(2):
            kept_ref[first + half] = now_refs[half][...]

    strips = range(2 * PIECES[0][0], 2 * PIECES[0][1])
    each_pair(strips, fill, list_ref, cos_ref, sin_ref, acc_ref, f_ref, (g0, g1), (h0, h1), done)
    turn(tile_ref[1], acc_ref, send_ref, keep_ref)


def right_kernel(piece, tile_ref, cos_ref, sin_ref, list_ref, kept_ref, old_ref, send_ref, keep_ref, acc_ref):
    low, high = PIECES[piece]
    acc_ref[...] = old_ref[low * YR * STRIP : high * YR * STRIP, :]

    def one_pair(pair, carry):
        refs = kept_ref.at[2 * pair], kept_ref.at[2 * pair + 1]
        project(2 * pair, range(2 * low, 2 * high), list_ref, cos_ref, sin_ref, acc_ref, refs)
        return carry

    lax.fori_loop(0, (list_ref[0] + 1) // 2, one_pair, 0)
    turn(tile_ref[1], acc_ref, send_ref, keep_ref)


def half_kernel(chip_ref, keep_ref, got_ref, *refs):
    send_ref, rest_ref = refs[-2:]
    chip = chip_ref[0]
    mine = pl.ds(pl.multiple_of(chip * 64, 64), 64)
    theirs = pl.ds(pl.multiple_of((1 - chip) * 64, 64), 64)
    send_ref[...] = (keep_ref[theirs, :] + got_ref[theirs, :].astype(F32)).astype(BF16)
    rest_ref[...] = keep_ref[mine, :] + got_ref[mine, :].astype(F32)


def sum_kernel(piece, rest_ref, got_ref, *refs):
    out_ref, sum_ref, sem = refs[-3:]
    low, high = PIECES[piece]
    width = (high - low) * STRIP
    copies = []
    for y in range(YR):
        cols = pl.ds(y * width, width)
        sum_ref[:, cols] = rest_ref[:, cols] + got_ref[:, cols].astype(F32)
        place = out_ref.at[0, :, pl.ds(y * PIX + low * STRIP, width)]
        copies.append(pltpu.make_async_copy(sum_ref.at[:, cols], place, sem.at[y]))
        copies[-1].start()
    for copy in copies:
        copy.wait()


VMEM = pl.BlockSpec(memory_space=pltpu.VMEM)
SMEM = pl.BlockSpec(memory_space=pltpu.SMEM)
HBM = pl.BlockSpec(memory_space=pltpu.HBM)
LATER = pl.BlockSpec(memory_space=pl.ANY)


def stay(array):
    return pltpu.with_memory_space_constraint(array, pltpu.HBM)


def shape(dims, dtype):
    return jax.ShapeDtypeStruct(dims, dtype)


def cost(flops, moved):
    return pl.CostEstimate(flops=flops, bytes_accessed=moved, transcendentals=0)


LIMIT = 24 * 2**20
BLOCK_FLOPS = 2 * 4096 * 256 * 256 + 2 * CH * COLS * 512
PIXELS = YR * PIX


def shards(raw_views, tap_channel, tap_view, tap_weight, batch_view, footprint, plane_weight):
    segment = lax.axis_index("segment")
    slab = lax.axis_index("slab")
    chip, core = segment // 2, segment % 2
    x_pos, y_hi, z_pos = slab // 8, slab // 4 % 2, slab % 4
    batch = jnp.bitwise_xor(chip, y_hi)

    def call(kernel, out_shape, in_specs, *operands, scratch=(), work=(10**5, 10**6), limit=LIMIT):
        many = isinstance(out_shape, tuple)
        return pl.pallas_call(
            kernel,
            out_shape=out_shape,
            in_specs=in_specs,
            out_specs=tuple(SMEM if o.dtype == jnp.int32 else VMEM for o in out_shape) if many else VMEM,
            scratch_shapes=list(scratch),
            compiler_params=pltpu.CompilerParams(vmem_limit_bytes=limit),
            cost_estimate=cost(*work),
        )(*operands)

    own, last, first = call(
        message_kernel,
        (shape((PAY, COLS), BF16), shape((CH // 2, COLS), BF16), shape((CH // 2, COLS), BF16)),
        [SMEM, HBM, HBM, HBM],
        batch[None],
        stay(footprint),
        stay(raw_views),
        stay(plane_weight),
        scratch=[
            pltpu.SMEM((2, 1, FOOT), jnp.int32),
            pltpu.VMEM((TZ, COLS), BF16),
            pltpu.SemaphoreType.DMA((3,)),
        ],
    )
    other = lax.ppermute(own, AXES, main_pairs())
    low = lax.ppermute(last, AXES, side_pairs(-1))
    high = lax.ppermute(first, AXES, side_pairs(1))

    prepared = call(
        prepare_kernel,
        (shape((CH, 3 * CHP), BF16), shape((CH, 1), F32), shape((CH, CHP), BF16)),
        [LATER, VMEM, VMEM, VMEM, HBM],
        own,
        stay(tap_channel),
        stay(tap_view),
        stay(tap_weight),
        stay(ramp_matrix()),
        scratch=[pltpu.SemaphoreType.DMA],
        work=(10**6, 4 * 10**6),
    )
    payload = call(
        filter_kernel,
        shape((PAY, COLS), BF16),
        [SMEM] + [VMEM] * 7,
        (core == y_hi).astype(jnp.int32)[None],
        own,
        other,
        low,
        high,
        *prepared,
        scratch=[pltpu.VMEM((3 * CHP, 2 * COLS), BF16), pltpu.VMEM((CHP, COLS), BF16)],
        work=(4 * 10**9, 4 * 10**6),
    )
    payload, batch_view = lax.optimization_barrier((payload, batch_view))
    got_a = lax.ppermute(payload, AXES, torus_pairs(*A1))
    got_b = lax.ppermute(payload, AXES, torus_pairs(*B1))
    got_c = lax.ppermute(payload, AXES, torus_pairs(*C1))
    blocks = lax.dynamic_index_in_dim(jnp.asarray(block_table()), x_pos * 4 + z_pos, 0, keepdims=False)
    first_view = lax.dynamic_index_in_dim(batch_view, batch, 0, keepdims=False)
    views = jnp.arange(32, dtype=jnp.int32)
    angle = first_view + 2 * (jnp.repeat(blocks, 2) + core * 4) + views % 2
    theta = angle.astype(F32) * (2.0 * math.pi / VPT)
    cos, sin = jnp.cos(theta), jnp.sin(theta)
    tile = jnp.where(jnp.arange(2) == 0, slab, core).astype(jnp.int32)

    two = shape((2, PAY, COLS), BF16)
    accumulator = shape((PIXELS, TZ), F32)
    total = call(
        own_kernel, accumulator, [SMEM] * 3 + [VMEM],
        tile, cos, sin, payload,
        scratch=[pltpu.VMEM((CH, 2 * TZ), BF16), pltpu.VMEM((1, CH + TZ, COLS), BF16), pltpu.SMEM((3,), jnp.int32)],
        work=(BLOCK_FLOPS, 10**6),
    )
    pairs = (
        call(pair_kernel, two, [VMEM, VMEM], payload, got_a),
        call(pair_kernel, two, [VMEM, VMEM, LATER], got_b, got_c, total),
    )
    near = [lax.ppermute(pairs[which], AXES, torus_pairs(even, odd)) for which, even, odd in NEAR]

    def scratch(count, listed=True):
        weighed = [pltpu.VMEM((CH, 2 * TZ), BF16)] * 4
        found = [pltpu.VMEM((count, CH + TZ, COLS), BF16)]
        return weighed + found + [pltpu.SMEM((1 + 2 * count,), jnp.int32)] * listed

    total = call(
        functools.partial(later_kernel, 1, 3), accumulator, [SMEM] * 3 + [VMEM] * 4,
        tile, cos, sin, got_a, got_b, got_c, total,
        scratch=scratch(3), work=(3 * BLOCK_FLOPS, 5 * 10**6),
    )
    far = []
    for arrival, which, even, odd in FAR:
        passed = call(
            functools.partial(pick_kernel, which), shape((PAY, COLS), BF16), [VMEM, LATER], near[arrival], total
        )
        far.append(lax.ppermute(passed, AXES, torus_pairs(even, odd)))
    total = call(
        functools.partial(later_kernel, 4, 4), accumulator, [SMEM] * 3 + [VMEM] * 5,
        tile, cos, sin, *near, total,
        scratch=scratch(8), work=(8 * BLOCK_FLOPS, 10**7),
    )
    beside = [(s * 32 + t, (s ^ 1) * 32 + t) for s in range(4) for t in range(32)]
    across = [(s * 32 + t, (s ^ 2) * 32 + t) for s in range(4) for t in range(32)]
    ends, before = [], []
    for piece, (first_strip, last_strip) in enumerate(PIECES):
        pixels = (last_strip - first_strip) * STRIP * YR
        outputs = (shape((COLS, pixels), BF16), shape((COLS, pixels), F32))
        acc = [pltpu.VMEM((pixels, TZ), F32)]
        if piece == 0:
            send, keep, kept, slots = call(
                left_kernel,
                outputs + (shape((4, CH, 2 * TZ), BF16), shape((9,), jnp.int32)),
                [SMEM] * 3 + [VMEM] * 5,
                tile, cos, sin, *far, total,
                scratch=acc + scratch(4, False), work=(2 * BLOCK_FLOPS, 9 * 10**6),
            )
        else:
            send, keep = call(
                functools.partial(right_kernel, piece),
                outputs,
                [SMEM] * 4 + [VMEM] * 2,
                tile, cos, sin, slots, kept, total,
                scratch=acc, work=(BLOCK_FLOPS, 4 * 10**6),
            )
        swapped = lax.ppermute(send, AXES, beside)
        send, rest = call(
            half_kernel,
            (shape((64, pixels), BF16), shape((64, pixels), F32)),
            [SMEM, VMEM, VMEM] + [LATER] * len(before),
            chip[None], keep, swapped, *before,
        )
        before = [send]
        ends.append((rest, lax.ppermute(send, AXES, across)))
    image = None
    for piece, (rest, swapped) in enumerate(ends):
        held = [image] if piece else []
        image = pl.pallas_call(
            functools.partial(sum_kernel, piece),
            out_shape=shape((1, 64, PIXELS), F32),
            in_specs=[VMEM, VMEM] + [LATER] * len(held),
            out_specs=LATER,
            scratch_shapes=[pltpu.VMEM(rest.shape, F32), pltpu.SemaphoreType.DMA((YR,))],
            input_output_aliases={2: 0} if held else {},
            compiler_params=pltpu.CompilerParams(vmem_limit_bytes=LIMIT),
            cost_estimate=cost(10**5, 10**6),
        )(rest, swapped, *held)
    return image


def solution(mesh):
    return jax.shard_map(
        shards,
        mesh=mesh,
        in_specs=(
            P(None, None, "slab"),
            P(),
            P(),
            P(),
            P(),
            P(None, "slab", None),
            P(None, "slab", None, None),
        ),
        out_specs=P("slab", "segment", None),
        check_vma=False,
    )
```

```python
import functools
import math

import jax
import jax.numpy as jnp
import numpy as np
from jax import lax
from jax.experimental import pallas as pl
from jax.experimental.pallas import tpu as pltpu
from jax.sharding import PartitionSpec as P

CH = 736
CHP = 768
ROWS = 64
COLS = 128
PIX = 1024
YR = 4
VPT = 1152
FOOT = 12
TZ = 256
PAY = CH + TZ + 16
STRIP = 128
STRIPS = PIX // STRIP
NARROW = 64
NARROWS = PIX // NARROW
PIECES = ((0, 4), (4, 8))
AXES = ("segment", "slab")
SCALE = CH / PIX
F32 = jnp.float32
BF16 = jnp.bfloat16


def linear(x, y, z, core):
    return ((y % 2) * 2 + core) * 32 + (x % 4) * 8 + (y // 2) * 4 + z % 4


def devices():
    for x in range(4):
        for y in range(4):
            for z in range(4):
                for core in range(2):
                    yield x, y, z, core


def home(slab, batch, core):
    x, y_hi, z = slab // 8, slab // 4 % 2, slab % 4
    return linear(x, batch if y_hi == 0 else 3 - batch, z, core)


def batch_of(y):
    return y % 2 ^ y // 2


def main_pairs():
    return [
        (home(x * 8 + core * 4 + z, batch_of(y), core), linear(x, y, z, core))
        for x, y, z, core in devices()
        if core != y // 2
    ]


def side_pairs(shift):
    pairs = []
    for x, y, z, core in devices():
        slab = x * 8 + core * 4 + z + shift
        if 0 <= slab < 32:
            pairs.append((home(slab, batch_of(y), y // 2), linear(x, y, z, core)))
    return pairs


def torus_pairs(even, odd):
    pairs = []
    for x, y, z, core in devices():
        dx, dz = odd if (x + z) % 2 else even
        pairs.append((linear(x + dx, y, z + dz, core), linear(x, y, z, core)))
    return pairs


A1, B1, C1 = ((2, 0), (0, 2)), ((0, 1), (1, 0)), ((0, -1), (-1, 0))
NEAR = (
    (0, (1, 0), (0, 1)),
    (0, (-1, 0), (0, -1)),
    (1, (0, 1), (1, 0)),
    (1, (0, -1), (-1, 0)),
)
FAR = (
    (0, 0, (0, 1), (1, 0)),
    (1, 1, (0, -1), (-1, 0)),
    (2, 0, (1, 0), (0, 1)),
    (3, 1, (-1, 0), (0, -1)),
)


def block_table():
    table = np.zeros((16, 16), np.int32)
    for x in range(4):
        for z in range(4):

            def first(px, pz):
                odd = (px + pz) % 2
                out = [(px, pz)]
                for offsets in (A1, B1, C1):
                    dx, dz = offsets[odd]
                    out.append((px + dx, pz + dz))
                return out

            found = first(x, z)

            def second(px, pz, arrival):
                which, even, odd = NEAR[arrival]
                dx, dz = odd if (px + pz) % 2 else even
                source = first(px + dx, pz + dz)
                return source[:2] if which == 0 else source[2:]

            for arrival in range(4):
                found += second(x, z, arrival)
            for arrival, which, even, odd in FAR:
                dx, dz = odd if (x + z) % 2 else even
                found.append(second(x + dx, z + dz, arrival)[which])
            found = [(px % 4, pz % 4) for px, pz in found]
            assert len(set(found)) == 16
            table[x * 4 + z] = [px * 8 + pz for px, pz in found]
    return table


def ramp_matrix():
    distance = np.arange(CH)[:, None] - np.arange(CHP)[None, :]
    odd = distance % 2 != 0
    taps = np.where(odd, -4.0 / (math.pi**2 * np.where(odd, distance, 1) ** 2.0), 0.0)
    taps = np.where(distance == 0, 1.0, taps) * (np.arange(CHP) < CH)
    return jnp.asarray(taps.astype(np.float32).astype(BF16))


def packed(view):
    return jnp.concatenate([view[: CH // 2], view[CH // 2 :]], axis=1)


def unpacked(ref):
    return jnp.concatenate([ref[:, :ROWS], ref[:, ROWS:]], axis=0)


def column(line):
    return jnp.broadcast_to(line.reshape(1, CH), (8, CH)).T[:, :1]


def message_kernel(batch_ref, feet_hbm, raw_hbm, weight_hbm, own_ref, last_ref, first_ref, feet_ref, flat_ref, sem):
    batch = batch_ref[0]
    copies = [
        pltpu.make_async_copy(raw_hbm.at[batch], own_ref.at[pl.ds(0, CH)], sem.at[0]),
        pltpu.make_async_copy(weight_hbm.at[batch, 0], flat_ref, sem.at[1]),
        pltpu.make_async_copy(feet_hbm, feet_ref, sem.at[2]),
    ]
    for copy in copies:
        copy.start()
    for copy in copies:
        copy.wait()
    row = lax.broadcasted_iota(jnp.int32, (16, COLS), 0)
    lane = lax.broadcasted_iota(jnp.int32, (16, COLS), 1)
    feet = jnp.full((16, COLS), -1.0, F32)
    for slot in range(FOOT):
        here = jnp.logical_and(row == 0, lane == slot)
        feet = jnp.where(here, feet_ref[batch, 0, slot].astype(F32), feet)
    own_ref[CH + TZ :, :] = feet.astype(BF16)
    own_ref[CH : CH + COLS, :] = flat_ref[:COLS, :].astype(F32).T.astype(BF16)
    own_ref[CH + COLS : CH + TZ, :] = flat_ref[COLS:, :].astype(F32).T.astype(BF16)
    raw = own_ref[:CH, :]
    last_ref[...] = packed(raw[:, ROWS:])
    first_ref[...] = packed(raw[:, :ROWS])


def pair_kernel(one_ref, two_ref, *refs):
    out_ref = refs[-1]
    out_ref[0] = one_ref[...]
    out_ref[1] = two_ref[...]


def pick_kernel(which, pair_ref, _, out_ref):
    out_ref[...] = pair_ref[which]


def prepare_kernel(_, channel_ref, view_ref, weight_ref, ramp_hbm, pick_ref, column_ref, ramp_ref, sem):
    copy = pltpu.make_async_copy(ramp_hbm, ramp_ref, sem)
    copy.start()
    column_ref[0] = column(weight_ref[...])
    column_ref[1] = column(view_ref[...].astype(F32))
    channel = lax.broadcasted_iota(jnp.int32, (CH, CHP), 1)
    pick_ref[...] = jnp.where(channel == column(channel_ref[...]), 1.0, 0.0).astype(BF16)
    copy.wait()


def filter_kernel(mine_ref, own_ref, other_ref, low_ref, high_ref, pick_ref, column_ref, ramp_ref, out_ref, x_ref, r_ref):
    keep = mine_ref[0] != 0
    both = jnp.where(keep, own_ref[...], other_ref[...])
    raw = both[:CH]
    low = jnp.concatenate([unpacked(low_ref), raw[:, :ROWS]], axis=1)
    high = jnp.concatenate([raw[:, ROWS:], unpacked(high_ref)], axis=1)
    x_ref[CH:, :] = jnp.zeros((CHP - CH, 6 * COLS), BF16)
    for tap, part in enumerate((low, raw, high)):
        up = jnp.concatenate([part[1:], part[:1]], axis=0)
        x_ref[:CH, pl.ds(tap * 2 * COLS, COLS)] = part
        x_ref[:CH, pl.ds((tap * 2 + 1) * COLS, COLS)] = up
    picked = jnp.dot(pick_ref[...], x_ref[...], preferred_element_type=F32)
    weight, view = column_ref[0], column_ref[1]
    lower, upper = (
        jnp.where(
            view == 0.0,
            picked[:, side : side + COLS],
            jnp.where(view == 1.0, picked[:, 256 + side : 384 + side], picked[:, 512 + side : 640 + side]),
        )
        for side in (0, COLS)
    )
    r_ref[:CH, :] = ((1.0 - weight) * lower + weight * upper).astype(BF16)
    r_ref[CH:, :] = jnp.zeros((CHP - CH, COLS), BF16)
    out_ref[:CH, :] = jnp.dot(ramp_ref[...], r_ref[...], preferred_element_type=F32).astype(BF16)
    out_ref[CH:, :] = both[CH:]


def stage(base, names, tile_ref, f_ref, list_ref):
    lane = lax.broadcasted_iota(jnp.int32, (16, COLS), 1)
    row = lax.broadcasted_iota(jnp.int32, (16, COLS), 0)
    slots = []
    for block in names:
        feet = block[CH + TZ :, :].astype(F32)
        hit = jnp.logical_and(feet == tile_ref[0].astype(F32), row == 0)
        slots.append(jnp.sum(jnp.where(hit, lane + 1, 0).astype(F32)).astype(jnp.int32))
    list_ref[0] = 0
    for index, (slot, block) in enumerate(zip(slots, names)):

        @pl.when(slot > 0)
        def _():
            found = list_ref[0]
            f_ref[found] = block[: CH + TZ, :]
            list_ref[1 + 2 * found] = slot - 1
            list_ref[2 + 2 * found] = base + index
            list_ref[0] = found + 1


def weigh(f_ref, found, g_ref):
    lane = lax.broadcasted_iota(jnp.int32, (CH, COLS), 1)
    values = f_ref[found, :CH, :]
    weight = jnp.concatenate([f_ref[found, CH : CH + COLS, :], f_ref[found, CH + COLS :, :]], axis=1)
    zero = jnp.zeros_like(values)
    for view in range(2):
        part = jnp.where((lane < ROWS) == (view == 0), values, zero)
        g_ref[:, pl.ds(view * TZ, TZ)] = jnp.dot(part, weight, preferred_element_type=F32).astype(BF16)


def project(first, strips, list_ref, cos_ref, sin_ref, acc_ref, g_refs):
    count = list_ref[0]
    lane = lax.broadcasted_iota(jnp.int32, (NARROW, COLS), 1)
    early = lane < NARROW
    x_iota = lax.broadcasted_iota(jnp.int32, (NARROW, COLS), 0).astype(F32)
    c_iota = jnp.where(early, lane, lane - NARROW).astype(F32)
    early = early[:8]
    blocks = []
    for half in range(2):
        found = jnp.minimum(first + half, count - 1)
        slot, number = list_ref[1 + 2 * found], list_ref[2 + 2 * found]
        shift = (slot.astype(F32) - (FOOT - 1) / 2.0) * (PIX / (4.0 * FOOT))
        y_first = shift - (YR / 2.0 - 0.5)
        cos = [cos_ref[2 * number + view] * SCALE for view in range(2)]
        sin = [sin_ref[2 * number + view] * SCALE for view in range(2)]
        slope = x_iota * jnp.where(lane < NARROW, cos[0], cos[1]) - c_iota
        reach = [
            jnp.minimum(0.0, (NARROW - 1) * cos[view]) + jnp.minimum(0.0, (YR - 1) * sin[view]) - 0.01
            for view in range(2)
        ]
        absent = jnp.where(first + half < count, 0.0, 4096.0)
        blocks.append((y_first, cos, sin, slope, reach, absent))
    zero, one = jnp.zeros((), BF16), jnp.ones((), BF16)
    for place, strip in enumerate(strips):
        x_first = strip * NARROW - (PIX / 2.0 - 0.5)
        windows, parts = [], []
        for (y_first, cos, sin, slope, reach, absent), g_ref in zip(blocks, g_refs):
            offset = []
            for view in range(2):
                u = (CH - 1) / 2.0 + x_first * cos[view] + y_first * sin[view]
                low = jnp.clip(u + reach[view], 0.0, float(CH - NARROW)).astype(jnp.int32)
                start = pl.multiple_of(lax.shift_left(lax.shift_right_logical(low, 4), 4), 16)
                offset.append(u - start.astype(F32) + absent)
                windows.append(g_ref[pl.ds(start, NARROW), pl.ds(view * TZ, TZ)])
            rows = []
            for y in range(YR):
                move = jnp.where(early, offset[0] + y * sin[0], offset[1] + y * sin[1])
                away = jnp.abs((slope + jnp.concatenate([move] * (NARROW // 8), axis=0)).astype(BF16))
                rows.append(jnp.maximum(zero, one - away))
            parts.append(jnp.concatenate(rows, axis=0))
        term = jnp.dot(
            jnp.concatenate(parts, axis=1),
            jnp.concatenate(windows, axis=0),
            preferred_element_type=F32,
        )
        for y in range(YR):
            row = place // 2 * (YR * STRIP) + y * STRIP + place % 2 * NARROW
            acc_ref[pl.ds(row, NARROW), :] += term[y * NARROW : (y + 1) * NARROW]


def each_pair(strips, fill, list_ref, cos_ref, sin_ref, acc_ref, f_ref, now, later, done=None):
    count = list_ref[0]

    def weigh_pair(first, g_refs):
        for half in range(2):
            weigh(f_ref, jnp.minimum(first + half, count - 1), g_refs[half])

    def step(first, now_refs, next_refs):
        weigh_pair(first + 2, next_refs)
        project(first, strips, list_ref, cos_ref, sin_ref, acc_ref, now_refs)
        if done is not None:
            done(first, now_refs)

    @pl.when(count > 0)
    def _():
        weigh_pair(0, now)
        fill()

    @pl.when(count == 0)
    def _():
        fill()

    def four(index, carry):
        step(4 * index, now, later)

        @pl.when(4 * index + 2 < count)
        def _():
            step(4 * index + 2, later, now)

        return carry

    lax.fori_loop(0, (count + 3) // 4, four, 0)


def own_kernel(tile_ref, cos_ref, sin_ref, block_ref, acc_ref, g_ref, f_ref, list_ref):
    stage(0, [block_ref], tile_ref, f_ref, list_ref)

    def fill():
        acc_ref[...] = jnp.zeros_like(acc_ref)

    @pl.when(list_ref[0] > 0)
    def _():
        weigh(f_ref, 0, g_ref)
        fill()
        project(0, range(NARROWS), list_ref, cos_ref, sin_ref, acc_ref, (g_ref, g_ref))

    @pl.when(list_ref[0] == 0)
    def _():
        fill()


def later_kernel(base, size, tile_ref, cos_ref, sin_ref, *refs):
    names = []
    for ref in refs[:size]:
        names += [ref] if len(ref.shape) == 2 else [ref.at[0], ref.at[1]]
    old_ref, acc_ref, g0, g1, h0, h1, f_ref, list_ref = refs[size:]
    stage(base, names, tile_ref, f_ref, list_ref)

    def fill():
        acc_ref[...] = old_ref[...]

    each_pair(range(NARROWS), fill, list_ref, cos_ref, sin_ref, acc_ref, f_ref, (g0, g1), (h0, h1))


def turn(core, acc_ref, send_ref, keep_ref):
    width = acc_ref.shape[0] // YR

    def one_strip(strip, carry):
        for y in range(YR):
            rows = pl.ds(pl.multiple_of(strip * (YR * STRIP) + y * STRIP, STRIP), STRIP)
            turned = acc_ref[rows, :].T
            cols = pl.ds(pl.multiple_of(strip * STRIP + y * width, STRIP), STRIP)
            keep_ref[:64, cols] = jnp.where(core == 0, turned[:64], turned[64:128])
            keep_ref[64:, cols] = jnp.where(core == 0, turned[128:192], turned[192:])
            send_ref[:64, cols] = jnp.where(core == 0, turned[64:128], turned[:64]).astype(BF16)
            send_ref[64:, cols] = jnp.where(core == 0, turned[192:], turned[128:192]).astype(BF16)
        return carry

    lax.fori_loop(0, width // STRIP, one_strip, 0)


def left_kernel(tile_ref, cos_ref, sin_ref, *refs):
    old_ref, send_ref, keep_ref, kept_ref, list_ref, acc_ref, g0, g1, h0, h1, f_ref = refs[4:]
    stage(12, refs[:4], tile_ref, f_ref, list_ref)

    def fill():
        acc_ref[...] = old_ref[: acc_ref.shape[0], :]

    def done(first, now_refs):
        for half in range(2):
            kept_ref[first + half] = now_refs[half][...]

    strips = range(2 * PIECES[0][0], 2 * PIECES[0][1])
    each_pair(strips, fill, list_ref, cos_ref, sin_ref, acc_ref, f_ref, (g0, g1), (h0, h1), done)
    turn(tile_ref[1], acc_ref, send_ref, keep_ref)


def right_kernel(piece, tile_ref, cos_ref, sin_ref, list_ref, kept_ref, old_ref, send_ref, keep_ref, acc_ref):
    low, high = PIECES[piece]
    acc_ref[...] = old_ref[low * YR * STRIP : high * YR * STRIP, :]

    def one_pair(pair, carry):
        refs = kept_ref.at[2 * pair], kept_ref.at[2 * pair + 1]
        project(2 * pair, range(2 * low, 2 * high), list_ref, cos_ref, sin_ref, acc_ref, refs)
        return carry

    lax.fori_loop(0, (list_ref[0] + 1) // 2, one_pair, 0)
    turn(tile_ref[1], acc_ref, send_ref, keep_ref)


def half_kernel(chip_ref, keep_ref, got_ref, *refs):
    send_ref, rest_ref = refs[-2:]
    chip = chip_ref[0]
    mine = pl.ds(pl.multiple_of(chip * 64, 64), 64)
    theirs = pl.ds(pl.multiple_of((1 - chip) * 64, 64), 64)
    send_ref[...] = (keep_ref[theirs, :] + got_ref[theirs, :].astype(F32)).astype(BF16)
    rest_ref[...] = keep_ref[mine, :] + got_ref[mine, :].astype(F32)


def sum_kernel(piece, rest_ref, got_ref, *refs):
    out_ref, sum_ref, sem = refs[-3:]
    low, high = PIECES[piece]
    width = (high - low) * STRIP
    copies = []
    for y in range(YR):
        cols = pl.ds(y * width, width)
        sum_ref[:, cols] = rest_ref[:, cols] + got_ref[:, cols].astype(F32)
        place = out_ref.at[0, :, pl.ds(y * PIX + low * STRIP, width)]
        copies.append(pltpu.make_async_copy(sum_ref.at[:, cols], place, sem.at[y]))
        copies[-1].start()
    for copy in copies:
        copy.wait()


VMEM = pl.BlockSpec(memory_space=pltpu.VMEM)
SMEM = pl.BlockSpec(memory_space=pltpu.SMEM)
HBM = pl.BlockSpec(memory_space=pltpu.HBM)
LATER = pl.BlockSpec(memory_space=pl.ANY)


def stay(array):
    return pltpu.with_memory_space_constraint(array, pltpu.HBM)


def shape(dims, dtype):
    return jax.ShapeDtypeStruct(dims, dtype)


def cost(flops, moved):
    return pl.CostEstimate(flops=flops, bytes_accessed=moved, transcendentals=0)


LIMIT = 24 * 2**20
BLOCK_FLOPS = 2 * 4096 * 256 * 256 + 2 * CH * COLS * 512
PIXELS = YR * PIX


def shards(raw_views, tap_channel, tap_view, tap_weight, batch_view, footprint, plane_weight):
    segment = lax.axis_index("segment")
    slab = lax.axis_index("slab")
    chip, core = segment // 2, segment % 2
    x_pos, y_hi, z_pos = slab // 8, slab // 4 % 2, slab % 4
    batch = jnp.bitwise_xor(chip, y_hi)

    def call(kernel, out_shape, in_specs, *operands, scratch=(), work=(10**5, 10**6), limit=LIMIT):
        many = isinstance(out_shape, tuple)
        return pl.pallas_call(
            kernel,
            out_shape=out_shape,
            in_specs=in_specs,
            out_specs=tuple(SMEM if o.dtype == jnp.int32 else VMEM for o in out_shape) if many else VMEM,
            scratch_shapes=list(scratch),
            compiler_params=pltpu.CompilerParams(vmem_limit_bytes=limit),
            cost_estimate=cost(*work),
        )(*operands)

    own, last, first = call(
        message_kernel,
        (shape((PAY, COLS), BF16), shape((CH // 2, COLS), BF16), shape((CH // 2, COLS), BF16)),
        [SMEM, HBM, HBM, HBM],
        batch[None],
        stay(footprint),
        stay(raw_views),
        stay(plane_weight),
        scratch=[
            pltpu.SMEM((2, 1, FOOT), jnp.int32),
            pltpu.VMEM((TZ, COLS), BF16),
            pltpu.SemaphoreType.DMA((3,)),
        ],
    )
    other = lax.ppermute(own, AXES, main_pairs())
    low = lax.ppermute(last, AXES, side_pairs(-1))
    high = lax.ppermute(first, AXES, side_pairs(1))

    prepared = call(
        prepare_kernel,
        (shape((CH, CHP), BF16), shape((2, CH, 1), F32), shape((CH, CHP), BF16)),
        [LATER, VMEM, VMEM, VMEM, HBM],
        own,
        stay(tap_channel),
        stay(tap_view),
        stay(tap_weight),
        stay(ramp_matrix()),
        scratch=[pltpu.SemaphoreType.DMA],
        work=(10**6, 4 * 10**6),
    )
    payload = call(
        filter_kernel,
        shape((PAY, COLS), BF16),
        [SMEM] + [VMEM] * 7,
        (core == y_hi).astype(jnp.int32)[None],
        own,
        other,
        low,
        high,
        *prepared,
        scratch=[pltpu.VMEM((CHP, 6 * COLS), BF16), pltpu.VMEM((CHP, COLS), BF16)],
        work=(4 * 10**9, 4 * 10**6),
    )
    payload, batch_view = lax.optimization_barrier((payload, batch_view))
    got_a = lax.ppermute(payload, AXES, torus_pairs(*A1))
    got_b = lax.ppermute(payload, AXES, torus_pairs(*B1))
    got_c = lax.ppermute(payload, AXES, torus_pairs(*C1))
    blocks = lax.dynamic_index_in_dim(jnp.asarray(block_table()), x_pos * 4 + z_pos, 0, keepdims=False)
    first_view = lax.dynamic_index_in_dim(batch_view, batch, 0, keepdims=False)
    views = jnp.arange(32, dtype=jnp.int32)
    angle = first_view + 2 * (jnp.repeat(blocks, 2) + core * 4) + views % 2
    theta = angle.astype(F32) * (2.0 * math.pi / VPT)
    cos, sin = jnp.cos(theta), jnp.sin(theta)
    tile = jnp.where(jnp.arange(2) == 0, slab, core).astype(jnp.int32)

    two = shape((2, PAY, COLS), BF16)
    accumulator = shape((PIXELS, TZ), F32)
    total = call(
        own_kernel, accumulator, [SMEM] * 3 + [VMEM],
        tile, cos, sin, payload,
        scratch=[pltpu.VMEM((CH, 2 * TZ), BF16), pltpu.VMEM((1, CH + TZ, COLS), BF16), pltpu.SMEM((3,), jnp.int32)],
        work=(BLOCK_FLOPS, 10**6),
    )
    pairs = (
        call(pair_kernel, two, [VMEM, VMEM], payload, got_a),
        call(pair_kernel, two, [VMEM, VMEM, LATER], got_b, got_c, total),
    )
    near = [lax.ppermute(pairs[which], AXES, torus_pairs(even, odd)) for which, even, odd in NEAR]

    def scratch(count, listed=True):
        weighed = [pltpu.VMEM((CH, 2 * TZ), BF16)] * 4
        found = [pltpu.VMEM((count, CH + TZ, COLS), BF16)]
        return weighed + found + [pltpu.SMEM((1 + 2 * count,), jnp.int32)] * listed

    total = call(
        functools.partial(later_kernel, 1, 3), accumulator, [SMEM] * 3 + [VMEM] * 4,
        tile, cos, sin, got_a, got_b, got_c, total,
        scratch=scratch(3), work=(3 * BLOCK_FLOPS, 5 * 10**6),
    )
    far = []
    for arrival, which, even, odd in FAR:
        passed = call(
            functools.partial(pick_kernel, which), shape((PAY, COLS), BF16), [VMEM, LATER], near[arrival], total
        )
        far.append(lax.ppermute(passed, AXES, torus_pairs(even, odd)))
    total = call(
        functools.partial(later_kernel, 4, 4), accumulator, [SMEM] * 3 + [VMEM] * 5,
        tile, cos, sin, *near, total,
        scratch=scratch(8), work=(8 * BLOCK_FLOPS, 10**7),
    )
    beside = [(s * 32 + t, (s ^ 1) * 32 + t) for s in range(4) for t in range(32)]
    across = [(s * 32 + t, (s ^ 2) * 32 + t) for s in range(4) for t in range(32)]
    ends, before = [], []
    for piece, (first_strip, last_strip) in enumerate(PIECES):
        pixels = (last_strip - first_strip) * STRIP * YR
        outputs = (shape((COLS, pixels), BF16), shape((COLS, pixels), F32))
        acc = [pltpu.VMEM((pixels, TZ), F32)]
        if piece == 0:
            send, keep, kept, slots = call(
                left_kernel,
                outputs + (shape((4, CH, 2 * TZ), BF16), shape((9,), jnp.int32)),
                [SMEM] * 3 + [VMEM] * 5,
                tile, cos, sin, *far, total,
                scratch=acc + scratch(4, False), work=(2 * BLOCK_FLOPS, 9 * 10**6),
            )
        else:
            send, keep = call(
                functools.partial(right_kernel, piece),
                outputs,
                [SMEM] * 4 + [VMEM] * 2,
                tile, cos, sin, slots, kept, total,
                scratch=acc, work=(BLOCK_FLOPS, 4 * 10**6),
            )
        swapped = lax.ppermute(send, AXES, beside)
        send, rest = call(
            half_kernel,
            (shape((64, pixels), BF16), shape((64, pixels), F32)),
            [SMEM, VMEM, VMEM] + [LATER] * len(before),
            chip[None], keep, swapped, *before,
        )
        before = [send]
        ends.append((rest, lax.ppermute(send, AXES, across)))
    image = None
    for piece, (rest, swapped) in enumerate(ends):
        held = [image] if piece else []
        image = pl.pallas_call(
            functools.partial(sum_kernel, piece),
            out_shape=shape((1, 64, PIXELS), F32),
            in_specs=[VMEM, VMEM] + [LATER] * len(held),
            out_specs=LATER,
            scratch_shapes=[pltpu.VMEM(rest.shape, F32), pltpu.SemaphoreType.DMA((YR,))],
            input_output_aliases={2: 0} if held else {},
            compiler_params=pltpu.CompilerParams(vmem_limit_bytes=LIMIT),
            cost_estimate=cost(10**5, 10**6),
        )(rest, swapped, *held)
    return image


def solution(mesh):
    return jax.shard_map(
        shards,
        mesh=mesh,
        in_specs=(
            P(None, None, "slab"),
            P(),
            P(),
            P(),
            P(),
            P(None, "slab", None),
            P(None, "slab", None, None),
        ),
        out_specs=P("slab", "segment", None),
        check_vma=False,
    )
```
